512 devices in a mesh: sector: 16 (over y, x), grp: 32 (over z, core).
Axes of the slice: x: 4, y: 4, z: 16, core: 2. Of those that a mesh axis runs over, the one named last changes fastest.
Arguments:
- start_vector: bfloat16 [8192, 512], P(('sector', 'grp')), may hold values from -130 to 130
- tile_live: int32 [64], P('sector'), may hold values from 32 to 128, as said below
- env_blocks: bfloat16 [64, 384, 128, 128], P('grp', 'sector'), may hold values from -2 to 4
- block_owner: int32 [64, 384, 1], P('grp', 'sector'), may hold values from 0 to 15; in each aligned block of 24 rows (0 to 23, 24 to 47, ..., all dimensions but the last counted through in order) at most 2 rows name the same one
- block_rows: int32 [64, 384], P('grp', 'sector'), may hold values from 0 to 3
- block_cols: int32 [64, 384], P('grp', 'sector'), may hold values from 0 to 3
- site_left: bfloat16 [64, 1024], P('grp'), may hold values from -0.375 to 0.375
- mpo_pattern: int32 [64, 64], P('grp'), may hold values 0 or 1
- site_right: bfloat16 [64, 1024], P('grp'), may hold values from -0.375 to 0.375
- right_env: bfloat16 [64, 1024], P('grp'), may hold values from -0.125 to 0.125
Outputs:
- first_product: bfloat16 [8192, 512], P(('sector', 'grp'))
- second_product: bfloat16 [8192, 512], P(('sector', 'grp'))
The draws below stay inside these ranges and needn't reach their ends.
Inputs may be any that keep to these rules, and one draw needn't show every extreme that they name: `tile_live`: rows beyond a tile's live count are padding; some tile is full. `block_owner`: in each aligned block of 24 entries of one channel (the blocks one device holds), no owner is named more than 2 times.
All inputs are finite; a program needn't handle non-finite values. No bound on the sum of `mpo_pattern` on one device may be relied on, other than what follows from the above.
Results may differ from the reference program's by a relative error of at most 0.03.
Values may be sent and summed in bfloat16 or wider, within the bound.
A program may use at most 64 MiB of HBM per device.

```python
import math
import jax
import jax.numpy as jnp
import numpy as np
from jax import lax

WM = 64
D1 = 4
RB = 32
TR = 128
TPO = 4
CAP = 2
PHYS = 16
NCOL = 512
EB = 24
NBLK = 384
NT = 64
NROWS = 8192
N_SECTOR = 16


def draw_start_vector(key, part):
    key_noise, key_rows, key_cols = jax.random.split(key, 3)
    position = jnp.arange(NROWS, dtype=jnp.float32) / NROWS
    noise_part = jax.random.truncated_normal(key_noise, -4.0, 4.0, (NROWS, NCOL), jnp.float32)
    rising = 1.0 + 2.0 * position
    row_scale = jnp.exp(jax.random.uniform(key_rows, (NROWS,), jnp.float32, 0.0, math.log(10.0))) / 4.0
    col_scale = jnp.exp(jax.random.uniform(key_cols, (NCOL,), jnp.float32, 0.0, math.log(10.0))) / 4.0
    return (noise_part * (rising * row_scale)[:, None] * col_scale[None, :]).astype(jnp.bfloat16)


def draw_env_blocks(key, part):
    key_noise, key_diag = jax.random.split(key)
    block_shape = (WM, NBLK, TR, TR)
    noise_part = jax.random.truncated_normal(key_noise, -4.0, 4.0, block_shape, jnp.float32)
    identity = (jnp.arange(TR)[:, None] == jnp.arange(TR)[None, :]).astype(jnp.float32)
    diagonal = jax.random.uniform(key_diag, (WM, NBLK, 1, TR), jnp.float32, 1.0, 2.0)
    weight = (TPO / EB) ** 0.5
    return (weight * (identity * diagonal + 0.8 * noise_part / TR ** 0.5)).astype(jnp.bfloat16)


def draw_tile_live(key, part):
    key_live, key_order = jax.random.split(jax.random.fold_in(key, 7))
    live_rows = jax.random.randint(key_live, (NT,), TR // 4, TR + 1, dtype=jnp.int32)
    shuffled = jax.random.permutation(key_order, NT)
    return live_rows.at[shuffled[0]].set(TR).at[shuffled[1]].set(TR // 4)


def touch_ends(entries, own_key, least, largest):
    longest = entries.shape.index(max(entries.shape))
    spots = []
    for shift in (0, 1):
        where = [jax.random.randint(jax.random.fold_in(own_key, axis), (), 0, length) for axis, length in enumerate(entries.shape)]
        where[longest] = (where[longest] + shift) % entries.shape[longest]
        spots.append(tuple(where))
    return entries.at[spots[0]].set(least).at[spots[1]].set(largest)


def steps_of(key, dims, cuts, least, top_value):
    loudness, own = 1.0, jax.random.fold_in(key, 6)
    for dim, parts in cuts:
        steps = jnp.exp(jax.random.uniform(jax.random.fold_in(own, dim), (parts,), jnp.float32, least / len(cuts), top_value / len(cuts)))
        loudness = loudness * jnp.repeat(steps, dims[dim] // parts).reshape([-1 if axis == dim else 1 for axis in range(len(dims))])
    return loudness


def assign_block(stream_key, own, number, rows, number_of, top, limit, skew):
    order = jax.random.permutation(stream_key, number_of)
    heavy_load, common = shares(number_of, rows * top, limit, skew, True), shares(number_of, rows * top, limit, skew, False)
    places = jnp.arange(number_of)

    def named(tallies, rotation):
        used = int((tallies > 0).sum())
        fixed = max(1, used // 4)
        shifted = fixed + (places - fixed + rotation * (used - fixed)) % max(1, number_of - fixed)
        return jnp.zeros((number_of,), jnp.int32).at[order[jnp.where(places < fixed, places, shifted)]].set(jnp.asarray(tallies, jnp.int32))

    tallies = jnp.where(number % 4 == 0, named(heavy_load, number // 4), named(common, number - number // 4 - 1))
    mixed = jax.random.permutation(jax.random.fold_in(own, 3), number_of)
    giver, receiver = mixed[0:number_of // 2 * 2:2], mixed[1:number_of // 2 * 2:2]
    slack = jnp.minimum(tallies[giver] - 1, limit - tallies[receiver]) // 2
    slack = jnp.where((giver == order[0]) | (receiver == order[0]) | (tallies[receiver] == 0), 0, jnp.maximum(slack, 0))
    shifted = jax.random.randint(jax.random.fold_in(own, 4), (number_of // 2,), 0, 1 << 20) % (slack + 1)
    tallies = tallies.at[giver].add(-shifted).at[receiver].add(shifted)
    items = jnp.searchsorted(jnp.cumsum(tallies), jnp.arange(rows * top), side="right").astype(jnp.int32)
    listing = items.reshape(top, rows).T
    listing = listing[jax.random.permutation(jax.random.fold_in(own, 1), rows)]
    rotation = jax.random.randint(jax.random.fold_in(own, 2), (rows, 1), 0, top)
    return jnp.take_along_axis(listing, (jnp.arange(top)[None, :] + rotation) % top, axis=1)


def shares(number_of, total, most, slope, full):
    weights = [(1 << 20) // math.isqrt(standing ** slope) + 1 for standing in range(1, number_of + 1)]
    largest = most if full else min(most, max(-(-total // number_of), total * weights[0] // sum(weights)))
    least = 1 if total - largest >= number_of - 1 else 0
    counts, rest = [largest] + [least] * (number_of - 1), total - largest - least * (number_of - 1)
    while rest > 0:
        candidates = [i for i in range(1, number_of) if counts[i] < largest] or [i for i in range(1, number_of) if counts[i] < most]
        pool, remaining = sum([weights[i] for i in candidates]), rest
        for i in candidates:
            addition = min(most - counts[i], max(1, remaining * weights[i] // pool), rest)
            counts[i] = counts[i] + addition
            rest = rest - addition
    return np.array(counts)


def bell_draw(key, shape, spread, limit, cuts=(), held_as=jnp.bfloat16):
    loudness = steps_of(key, shape, cuts, -0.22, 0.18) if cuts else 1.0
    values = jax.random.normal(key, shape, jnp.float32) * spread * loudness
    return jnp.minimum(jnp.maximum(values, -limit), limit).astype(held_as)


def setup_inputs(seed: int = 0) -> dict:
    seeds = jax.random.split(jax.random.key(seed), 11)
    start_vector = draw_start_vector(jax.random.fold_in(seeds[10], 71), 0)
    tile_live = draw_tile_live(jax.random.fold_in(seeds[10], 71), 0)
    env_blocks = draw_env_blocks(jax.random.fold_in(seeds[10], 71), 0)
    block_owner_keys = jax.random.split(jax.random.fold_in(seeds[3], 1), WM * NBLK // EB)
    block_owner_turns = jax.random.permutation(jax.random.fold_in(seeds[3], 3), WM * NBLK // EB)
    block_owner = jax.vmap(lambda own, number: assign_block(jax.random.fold_in(seeds[3], 2), own, number, EB, N_SECTOR, 1, CAP, 2))(block_owner_keys, block_owner_turns).reshape((WM, NBLK, 1))
    block_rows = touch_ends(jax.random.randint(seeds[4], (WM, NBLK), 0, TPO), jax.random.fold_in(seeds[4], 1), 0, TPO - 1).astype(jnp.int32)
    block_cols = touch_ends(jax.random.randint(seeds[5], (WM, NBLK), 0, TPO), jax.random.fold_in(seeds[5], 1), 0, TPO - 1).astype(jnp.int32)
    site_left = bell_draw(seeds[6], (WM, WM * PHYS), (WM * D1) ** -0.5, 0.375, ((0, 32),))
    mpo_pattern = touch_ends((jax.random.randint(seeds[7], (WM, WM), 0, 2) < 1).astype(jnp.int32), jax.random.fold_in(seeds[7], 1), 0, 1)
    site_right = bell_draw(seeds[8], (WM, WM * PHYS), (WM * D1) ** -0.5, 0.375, ((0, 32),))
    right_env = bell_draw(seeds[9], (WM, RB * RB), (WM * RB) ** -0.5, 0.125, ((0, 32),))
    return {"start_vector": start_vector, "tile_live": tile_live, "env_blocks": env_blocks, "block_owner": block_owner, "block_rows": block_rows, "block_cols": block_cols, "site_left": site_left, "mpo_pattern": mpo_pattern, "site_right": site_right, "right_env": right_env}


epsilon = 1e-06

def build_mixing(site_left, mpo_pattern, site_right, right_env):
    left_site = site_left.reshape(WM, WM, D1, D1) * mpo_pattern.astype(jnp.bfloat16)[:, :, None, None]
    right_site = site_right.reshape(WM, WM, D1, D1)
    joined = jnp.einsum('wmac,mxbd->wxabcd', left_site.astype(jnp.float32), right_site.astype(jnp.float32)).astype(jnp.bfloat16)
    mixing = jnp.einsum('wxq,xr->wqr', joined.reshape(WM, WM, PHYS * PHYS).astype(jnp.float32), right_env.astype(jnp.float32)).astype(jnp.bfloat16)
    return mixing.reshape(WM, PHYS, PHYS, RB, RB).transpose(0, 2, 3, 1, 4).reshape(WM, NCOL, NCOL)

def apply_ham(vector, env_blocks, source, target, mixing):
    vector_tiles = vector.reshape(NT, TR, NCOL)

    def one_channel(accumulated, inputs):
        blocks, source_row, target_row, mixing_row = inputs
        picked = jnp.take(vector_tiles, source_row, axis=0).astype(jnp.float32)
        product = jnp.einsum('prk,pkn->prn', blocks.astype(jnp.float32), picked)
        mixed = jax.ops.segment_sum(product, target_row, num_segments=NT).reshape(NROWS, NCOL).astype(jnp.bfloat16)
        return (accumulated + jnp.dot(mixed, mixing_row, preferred_element_type=jnp.float32), None)
    accumulated, unused = lax.scan(one_channel, jnp.zeros((NROWS, NCOL), jnp.float32), (env_blocks, source, target, mixing))
    return accumulated

def reference(start_vector, tile_live, env_blocks, block_owner, block_rows, block_cols, site_left, mpo_pattern, site_right, right_env):
    row_mask = (jnp.arange(TR, dtype=jnp.int32)[None, :] < tile_live[:, None]).reshape(NROWS, 1)
    mixing = build_mixing(site_left, mpo_pattern, site_right, right_env)
    owners = block_owner[:, :, 0]
    source = (owners * TPO + block_cols).astype(jnp.int32)
    target = (owners * TPO + block_rows).astype(jnp.int32)
    masked_start = start_vector * row_mask.astype(jnp.bfloat16)
    first_product = (apply_ham(masked_start, env_blocks, source, target, mixing) * row_mask.astype(jnp.float32)).astype(jnp.bfloat16)
    widened = first_product.astype(jnp.float32)
    inverse_norm = lax.rsqrt(jnp.mean(widened * widened) + epsilon)
    direction = (widened * inverse_norm).astype(jnp.bfloat16)
    second_product = (apply_ham(direction, env_blocks, source, target, mixing) * row_mask.astype(jnp.float32)).astype(jnp.bfloat16)
    return (first_product, second_product)
```

```python
import jax
import jax.numpy as jnp
from jax import lax
from jax.sharding import PartitionSpec as P

WM = 64
D1 = 4
RB = 32
TR = 128
TPO = 4
CAP = 2
PHYS = 16


epsilon = 1e-06


def contract(owned_rows, got_blocks, got_codes):
    channels = got_blocks.shape[0]
    slot_count = got_blocks.shape[1] * got_blocks.shape[2]
    results = []
    for channel in range(channels):
        blocks = got_blocks[channel].reshape(slot_count, TR * TR)
        slot_codes = got_codes[channel].reshape(slot_count)
        tile_index = jnp.maximum(slot_codes - 1, 0)
        pair_hot = (
            (tile_index[:, None] == jnp.arange(TPO * TPO, dtype=jnp.int32)[None, :])
            & (slot_codes[:, None] > 0)
        ).astype(jnp.bfloat16)
        summed = jnp.einsum(
            "sp,sq->pq", pair_hot, blocks, preferred_element_type=jnp.float32
        ).astype(jnp.bfloat16)
        dense = summed.reshape(TPO, TPO, TR, TR).transpose(0, 2, 1, 3).reshape(TPO * TR, TPO * TR)
        product = jnp.dot(dense, owned_rows, preferred_element_type=jnp.float32)
        results.append(product.astype(jnp.bfloat16))
    return jnp.stack(results)


def owner_gather(share_rows):
    return lax.all_gather(share_rows, "grp", axis=0, tiled=True)


def channel_share(mixed_rows, mixing):
    return lax.psum_scatter(
        jnp.einsum("wrk,wkn->rn", mixed_rows, mixing, preferred_element_type=jnp.float32).astype(
            jnp.bfloat16
        ),
        "grp",
        scatter_dimension=0,
        tiled=True,
    ).astype(jnp.float32)


def local(
    start_vector,
    tile_live,
    env_blocks,
    block_owner,
    block_rows,
    block_cols,
    site_left,
    mpo_pattern,
    site_right,
    right_env,
):
    sectors = lax.axis_size("sector")
    groups = lax.axis_size("grp")
    share_count = start_vector.shape[0]
    columns = start_vector.shape[1]
    channels = env_blocks.shape[0]
    held_blocks = env_blocks.shape[1]
    right_site, right_panels = (
        lax.all_gather(site_right, "grp", axis=0, tiled=True),
        lax.all_gather(right_env, "grp", axis=0, tiled=True),
    )
    left_site = (
        site_left.reshape(channels, WM, D1, D1) * mpo_pattern.astype(jnp.bfloat16)[:, :, None, None]
    )
    joined = jnp.einsum(
        "wmac,mxbd->wxabcd",
        left_site,
        right_site.reshape(WM, WM, D1, D1),
        preferred_element_type=jnp.float32,
    ).astype(jnp.bfloat16)
    mixing = jnp.einsum(
        "wxq,xr->wqr",
        joined.reshape(channels, WM, PHYS * PHYS),
        right_panels,
        preferred_element_type=jnp.float32,
    ).astype(jnp.bfloat16)
    mixing = (
        mixing.reshape(channels, PHYS, PHYS, RB, RB)
        .transpose(0, 2, 3, 1, 4)
        .reshape(channels, columns, columns)
    )
    owners = block_owner[:, :, 0]
    owner_hot = (owners[:, :, None] == jnp.arange(sectors, dtype=jnp.int32)[None, None, :]).astype(
        jnp.int32
    )
    position = jnp.sum((jnp.cumsum(owner_hot, axis=1) - owner_hot) * owner_hot, axis=2)
    slot_index = owners * CAP + position
    select = slot_index[:, :, None] == jnp.arange(sectors * CAP, dtype=jnp.int32)[None, None, :]
    packed = jnp.einsum(
        "wes,wen->wsn",
        select.astype(jnp.bfloat16),
        env_blocks.reshape(channels, held_blocks, TR * TR),
        preferred_element_type=jnp.float32,
    ).astype(jnp.bfloat16)
    slot_codes = jnp.sum(
        select.astype(jnp.int32) * (1 + block_rows * TPO + block_cols)[:, :, None], axis=1
    )
    got_blocks, got_codes = (
        lax.all_to_all(
            packed.reshape(channels, sectors, CAP, TR * TR),
            "sector",
            split_axis=1,
            concat_axis=1,
            tiled=True,
        ),
        lax.all_to_all(
            slot_codes.reshape(channels, sectors, CAP),
            "sector",
            split_axis=1,
            concat_axis=1,
            tiled=True,
        ),
    )
    tile_mask = (jnp.arange(TR, dtype=jnp.int32)[None, :] < tile_live[:, None]).reshape(TPO * TR)
    owner_mask = tile_mask.astype(jnp.float32)[:, None]
    share_mask = lax.dynamic_slice_in_dim(
        owner_mask, lax.axis_index("grp") * share_count, share_count, 0
    )
    entry_count = float(sectors * groups * share_count * columns)
    owned_rows = owner_gather(start_vector) * owner_mask.astype(jnp.bfloat16)
    first_mixed = contract(owned_rows, got_blocks, got_codes)
    owner_total = lax.psum(
        jnp.einsum("wrk,wkn->rn", first_mixed, mixing, preferred_element_type=jnp.float32).astype(
            jnp.bfloat16
        ),
        "grp",
    ).astype(jnp.float32)
    owner_first = (owner_total * owner_mask).astype(jnp.bfloat16)
    first_product = lax.dynamic_slice_in_dim(
        owner_first, lax.axis_index("grp") * share_count, share_count, 0
    )
    widened = first_product.astype(jnp.float32)
    squares = lax.psum(jnp.sum(widened * widened), ("sector", "grp"))
    inverse_norm = lax.rsqrt(squares / entry_count + epsilon)
    second_mixed = contract(owner_first, got_blocks, got_codes)
    second_product = (channel_share(second_mixed, mixing) * inverse_norm * share_mask).astype(jnp.bfloat16)
    return (first_product, second_product)


def solution(mesh):
    in_specs = (
        P(("sector", "grp"), None),
        P("sector"),
        P("grp", "sector", None, None),
        P("grp", "sector", None),
        P("grp", "sector"),
        P("grp", "sector"),
        P("grp", None),
        P("grp", None),
        P("grp", None),
        P("grp", None),
    )
    out_specs = (P(("sector", "grp"), None), P(("sector", "grp"), None))
    return jax.shard_map(local, mesh=mesh, in_specs=in_specs, out_specs=out_specs, check_vma=False)
```

```python
import functools

import jax
import jax.numpy as jnp
from jax import lax
from jax.experimental import pallas as pl
from jax.experimental.pallas import tpu as pltpu
from jax.sharding import PartitionSpec as P

WM = 64
D1 = 4
RB = 32
TR = 128
TPO = 4
CAP = 2
PHYS = 16


epsilon = 1e-06


MESH = pl.DeviceIdType.MESH
SHARE = 16


def send_to(src, dst, send_sem, recv_sem, target):
    return pltpu.make_async_remote_copy(
        src_ref=src,
        dst_ref=dst,
        send_sem=send_sem,
        recv_sem=recv_sem,
        device_id=target,
        device_id_type=MESH,
    )


def greet(chips, chip, core, sectors=0):
    barrier = pltpu.get_barrier_semaphore()

    def greet_chip(step, carry):
        other = lax.rem(chip + step, chips)
        pl.semaphore_signal(
            barrier, inc=1, device_id={"grp": other * 2 + core}, device_id_type=MESH
        )
        return carry

    lax.fori_loop(1, chips, greet_chip, 0)
    pl.semaphore_signal(
        barrier, inc=1, device_id={"grp": chip * 2 + 1 - core}, device_id_type=MESH
    )
    if sectors:
        owner = lax.axis_index("sector")

        def greet_owner(step, carry):
            pl.semaphore_signal(
                barrier,
                inc=1,
                device_id={"sector": lax.rem(owner + step, sectors)},
                device_id_type=MESH,
            )
            return carry

        lax.fori_loop(1, sectors, greet_owner, 0)
        pl.semaphore_wait(barrier, chips + sectors - 1)
    else:
        pl.semaphore_wait(barrier, chips)


def spread(held, chips, chip, core, send_sem, recv_sem, pair_send, pair_recv):
    sibling = {"grp": chip * 2 + 1 - core}
    mine = held.at[chip, core]

    def outgoing(step):
        other = lax.rem(chip + step, chips)
        return send_to(
            mine, mine, send_sem.at[step], recv_sem.at[step], {"grp": other * 2 + core}
        )

    def forward(step):
        source = lax.rem(chip + chips - step, chips)
        block = held.at[source, core]
        return send_to(block, block, pair_send.at[step], pair_recv.at[step], sibling)

    def start(step, carry):
        outgoing(step).start()
        return carry

    def relay(step, carry):
        outgoing(step).wait_recv()
        forward(step).start()
        return carry

    def finish(step, carry):
        outgoing(step).wait_send()
        return carry

    def finish_pair(step, carry):
        forward(step).wait()
        return carry

    lax.fori_loop(1, chips, start, 0)
    forward(0).start()
    lax.fori_loop(1, chips, relay, 0)
    lax.fori_loop(1, chips, finish, 0)
    lax.fori_loop(0, chips, finish_pair, 0)


def gather_kernel(chips, rows_ref, site_ref, env_ref, rows_out, site_out, env_out, *sems):
    position = lax.axis_index("grp")
    chip, core = position // 2, lax.rem(position, 2)
    send_sem, recv_sem, pair_send, pair_recv = sems
    pairs = ((rows_ref, rows_out), (site_ref, site_out), (env_ref, env_out))
    for source, target in pairs:
        target[chip, core] = source[...]
    greet(chips, chip, core)
    sibling = {"grp": chip * 2 + 1 - core}

    def outgoing(item, step):
        other = lax.rem(chip + step, chips)
        mine = pairs[item][1].at[chip, core]
        return send_to(
            mine,
            mine,
            send_sem.at[item, step],
            recv_sem.at[item, step],
            {"grp": other * 2 + core},
        )

    def forward(item, step):
        source = lax.rem(chip + chips - step, chips)
        block = pairs[item][1].at[source, core]
        return send_to(block, block, pair_send.at[item, step], pair_recv.at[item, step], sibling)

    def start(step, carry):
        for item in (1, 2, 0):
            outgoing(item, step).start()
        return carry

    def relay(step, carry):
        for item in (1, 2, 0):
            outgoing(item, step).wait_recv()
            forward(item, step).start()
        return carry

    def finish(step, carry):
        for item in (1, 2, 0):
            outgoing(item, step).wait_send()
        return carry

    def finish_pair(step, carry):
        for item in (1, 2, 0):
            forward(item, step).wait()
        return carry

    lax.fori_loop(1, chips, start, 0)
    for item in (1, 2, 0):
        forward(item, 0).start()
    lax.fori_loop(1, chips, relay, 0)
    lax.fori_loop(1, chips, finish, 0)
    lax.fori_loop(0, chips, finish_pair, 0)


def gather_all(start_vector, site_right, right_env):
    chips = lax.axis_size("grp") // 2
    operands = (start_vector, site_right, right_env)
    return pl.pallas_call(
        functools.partial(gather_kernel, chips),
        out_shape=[jax.ShapeDtypeStruct((chips, 2) + a.shape, a.dtype) for a in operands],
        in_specs=[pl.BlockSpec(memory_space=pltpu.VMEM)] * 3,
        out_specs=[pl.BlockSpec(memory_space=pltpu.VMEM)] * 3,
        scratch_shapes=[pltpu.SemaphoreType.DMA((3, chips))] * 4,
        compiler_params=pltpu.CompilerParams(collective_id=0, has_side_effects=True),
    )(*operands)


def product(dense_ref, mix_ref, vector, part, base):
    tile = 256

    def one_tile(index, carry):
        rows = pl.ds(pl.multiple_of(index * tile, tile), tile)
        total = jnp.zeros((tile, vector.shape[1]), jnp.float32)
        for channel in range(dense_ref.shape[0]):
            mixed = jnp.dot(
                dense_ref[channel, rows, :], vector, preferred_element_type=jnp.float32
            ).astype(jnp.bfloat16)
            total += jnp.dot(mixed, mix_ref[channel], preferred_element_type=jnp.float32)
        split = total.astype(jnp.bfloat16).reshape(tile // (2 * SHARE), 2, SHARE, vector.shape[1])
        chunk = pl.ds(index * (tile // (2 * SHARE)), tile // (2 * SHARE))
        part[base, chunk] = split[:, 0]
        part[base + 1, chunk] = split[:, 1]
        return carry

    lax.fori_loop(0, TPO * TR // tile, one_tile, 0)


def reduce_share(chips, chip, core, part, base, sib, ready, got, sems):
    pair_send, pair_recv, send_sem, recv_sem = sems
    pair = send_to(
        part.at[base + 1 - core],
        sib,
        pair_send,
        pair_recv,
        {"grp": chip * 2 + 1 - core},
    )
    pair.start()
    pair.wait()
    ready[...] = (part[base + core].astype(jnp.float32) + sib[...].astype(jnp.float32)).astype(
        jnp.bfloat16
    )

    def outgoing(step):
        other = lax.rem(chip + step, chips)
        return send_to(
            ready.at[other],
            got.at[step],
            send_sem.at[step],
            recv_sem.at[step],
            {"grp": other * 2 + core},
        )

    def start(step, carry):
        outgoing(step).start()
        return carry

    def collect(step, total):
        outgoing(step).wait_recv()
        return total + got[step].astype(jnp.float32)

    def finish(step, carry):
        outgoing(step).wait_send()
        return carry

    lax.fori_loop(1, chips, start, 0)
    total = lax.fori_loop(1, chips, collect, ready[chip].astype(jnp.float32))
    lax.fori_loop(1, chips, finish, 0)
    return total


def step_kernel(
    chips,
    sectors,
    dense_ref,
    mix_ref,
    start_ref,
    mask_ref,
    first_out,
    second_out,
    part,
    sib_one,
    sib_two,
    ready_one,
    ready_two,
    got_one,
    got_two,
    held,
    norm_mine,
    norm_got,
    pair_sems,
    share_sems,
    spread_sems,
    norm_sems,
):
    position = lax.axis_index("grp")
    owner = lax.axis_index("sector")
    chip, core = position // 2, lax.rem(position, 2)
    rows = TPO * TR
    columns = start_ref.shape[-1]
    greet(chips, chip, core, sectors)
    masked = start_ref[...].reshape(rows, columns) * mask_ref[...].astype(jnp.bfloat16)
    product(dense_ref, mix_ref, masked, part, 0)
    share_mask = mask_ref[pl.ds(pl.multiple_of(position * SHARE, SHARE), SHARE), :]
    total = reduce_share(
        chips,
        chip,
        core,
        part,
        0,
        sib_one,
        ready_one,
        got_one,
        (pair_sems.at[0], pair_sems.at[1], share_sems.at[0], share_sems.at[1]),
    )
    first = (total * share_mask).astype(jnp.bfloat16)
    first_out[...] = first
    held[chip, core] = first
    spread(
        held,
        chips,
        chip,
        core,
        spread_sems.at[0],
        spread_sems.at[1],
        spread_sems.at[2],
        spread_sems.at[3],
    )
    wide = held[...].reshape(rows, columns).astype(jnp.float32)
    squares = jnp.sum((wide * wide).reshape(rows // 8, 8, columns), axis=0)
    norm_mine[...] = sum(squares[:, at : at + 128] for at in range(0, columns, 128))

    def norm_copy(step):
        return send_to(
            norm_mine,
            norm_got.at[step],
            norm_sems.at[0, step],
            norm_sems.at[1, step],
            {"sector": lax.rem(owner + step, sectors)},
        )

    def norm_start(step, carry):
        norm_copy(step).start()
        return carry

    def norm_collect(step, carry):
        norm_copy(step).wait()
        return carry + norm_got[step]

    lax.fori_loop(1, sectors, norm_start, 0)
    product(dense_ref, mix_ref, held[...].reshape(rows, columns), part, 2)
    total = reduce_share(
        chips,
        chip,
        core,
        part,
        2,
        sib_two,
        ready_two,
        got_two,
        (pair_sems.at[2], pair_sems.at[3], share_sems.at[2], share_sems.at[3]),
    )
    sums = lax.fori_loop(1, sectors, norm_collect, norm_mine[...])
    count = float(sectors * rows * columns)
    inverse_norm = lax.rsqrt(jnp.sum(sums, keepdims=True) / count + epsilon)
    second_out[...] = (total * inverse_norm * share_mask).astype(jnp.bfloat16)


def two_products(dense, mixing, owned_rows, owner_mask):
    chips = lax.axis_size("grp") // 2
    sectors = lax.axis_size("sector")
    columns = owned_rows.shape[-1]
    shares = pltpu.VMEM((chips, SHARE, columns), jnp.bfloat16)
    share = jax.ShapeDtypeStruct((SHARE, columns), jnp.bfloat16)
    return pl.pallas_call(
        functools.partial(step_kernel, chips, sectors),
        out_shape=[share, share],
        in_specs=[pl.BlockSpec(memory_space=pltpu.VMEM)] * 4,
        out_specs=[pl.BlockSpec(memory_space=pltpu.VMEM)] * 2,
        scratch_shapes=[
            pltpu.VMEM((4, chips, SHARE, columns), jnp.bfloat16),
            shares,
            shares,
            shares,
            shares,
            shares,
            shares,
            pltpu.VMEM((chips, 2, SHARE, columns), jnp.bfloat16),
            pltpu.VMEM((8, 128), jnp.float32),
            pltpu.VMEM((sectors, 8, 128), jnp.float32),
            pltpu.SemaphoreType.DMA((4,)),
            pltpu.SemaphoreType.DMA((4, chips)),
            pltpu.SemaphoreType.DMA((4, chips)),
            pltpu.SemaphoreType.DMA((2, sectors)),
        ],
        compiler_params=pltpu.CompilerParams(
            collective_id=1, has_side_effects=True, vmem_limit_bytes=40 * 1024 * 1024
        ),
    )(dense, mixing, owned_rows, owner_mask)


def assemble(got_blocks, got_codes):
    channels = got_blocks.shape[0]
    slot_count = got_blocks.shape[1] * got_blocks.shape[2]
    results = []
    for channel in range(channels):
        blocks = got_blocks[channel].reshape(slot_count, TR * TR)
        slot_codes = got_codes[channel].reshape(slot_count)
        tile_index = jnp.maximum(slot_codes - 1, 0)
        pair_hot = (
            (tile_index[:, None] == jnp.arange(TPO * TPO, dtype=jnp.int32)[None, :])
            & (slot_codes[:, None] > 0)
        ).astype(jnp.bfloat16)
        summed = jnp.einsum(
            "sp,sq->pq", pair_hot, blocks, preferred_element_type=jnp.float32
        ).astype(jnp.bfloat16)
        results.append(
            summed.reshape(TPO, TPO, TR, TR).transpose(0, 2, 1, 3).reshape(TPO * TR, TPO * TR)
        )
    return jnp.stack(results)


def local(
    start_vector,
    tile_live,
    env_blocks,
    block_owner,
    block_rows,
    block_cols,
    site_left,
    mpo_pattern,
    site_right,
    right_env,
):
    sectors = lax.axis_size("sector")
    columns = start_vector.shape[1]
    channels = env_blocks.shape[0]
    held_blocks = env_blocks.shape[1]
    owned_rows, right_site, right_panels = gather_all(start_vector, site_right, right_env)
    right_panels = right_panels.reshape(WM, RB * RB)
    left_site = (
        site_left.reshape(channels, WM, D1, D1) * mpo_pattern.astype(jnp.bfloat16)[:, :, None, None]
    )
    joined = jnp.einsum(
        "wmac,mxbd->wxabcd",
        left_site,
        right_site.reshape(WM, WM, D1, D1),
        preferred_element_type=jnp.float32,
    ).astype(jnp.bfloat16)
    mixing = jnp.einsum(
        "wxq,xr->wqr",
        joined.reshape(channels, WM, PHYS * PHYS),
        right_panels,
        preferred_element_type=jnp.float32,
    ).astype(jnp.bfloat16)
    mixing = (
        mixing.reshape(channels, PHYS, PHYS, RB, RB)
        .transpose(0, 2, 3, 1, 4)
        .reshape(channels, columns, columns)
    )
    owners = block_owner[:, :, 0]
    owner_hot = (owners[:, :, None] == jnp.arange(sectors, dtype=jnp.int32)[None, None, :]).astype(
        jnp.int32
    )
    position = jnp.sum((jnp.cumsum(owner_hot, axis=1) - owner_hot) * owner_hot, axis=2)
    slot_index = owners * CAP + position
    select = slot_index[:, :, None] == jnp.arange(sectors * CAP, dtype=jnp.int32)[None, None, :]
    packed = jnp.einsum(
        "wes,wen->wsn",
        select.astype(jnp.bfloat16),
        env_blocks.reshape(channels, held_blocks, TR * TR),
        preferred_element_type=jnp.float32,
    ).astype(jnp.bfloat16)
    slot_codes = jnp.sum(
        select.astype(jnp.int32) * (1 + block_rows * TPO + block_cols)[:, :, None], axis=1
    )
    got_blocks, got_codes = (
        lax.all_to_all(
            packed.reshape(channels, sectors, CAP, TR * TR),
            "sector",
            split_axis=1,
            concat_axis=1,
            tiled=True,
        ),
        lax.all_to_all(
            slot_codes.reshape(channels, sectors, CAP),
            "sector",
            split_axis=1,
            concat_axis=1,
            tiled=True,
        ),
    )
    tile_mask = (jnp.arange(TR, dtype=jnp.int32)[None, :] < tile_live[:, None]).reshape(TPO * TR)
    owner_mask = tile_mask.astype(jnp.float32)[:, None]
    return tuple(two_products(assemble(got_blocks, got_codes), mixing, owned_rows, owner_mask))


def solution(mesh):
    in_specs = (
        P(("sector", "grp"), None),
        P("sector"),
        P("grp", "sector", None, None),
        P("grp", "sector", None),
        P("grp", "sector"),
        P("grp", "sector"),
        P("grp", None),
        P("grp", None),
        P("grp", None),
        P("grp", None),
    )
    out_specs = (P(("sector", "grp"), None), P(("sector", "grp"), None))
    return jax.shard_map(local, mesh=mesh, in_specs=in_specs, out_specs=out_specs, check_vma=False)
```

```python
import functools

import jax
import jax.numpy as jnp
from jax import lax
from jax.experimental import pallas as pl
from jax.experimental.pallas import tpu as pltpu
from jax.sharding import PartitionSpec as P

WM = 64
D1 = 4
RB = 32
TR = 128
TPO = 4
CAP = 2
PHYS = 16


epsilon = 1e-06


MESH = pl.DeviceIdType.MESH
SHARE = 16


def send_to(src, dst, send_sem, recv_sem, target):
    return pltpu.make_async_remote_copy(
        src_ref=src,
        dst_ref=dst,
        send_sem=send_sem,
        recv_sem=recv_sem,
        device_id=target,
        device_id_type=MESH,
    )


def greet(chips, chip, core, sectors=0):
    barrier = pltpu.get_barrier_semaphore()

    def greet_chip(step, carry):
        other = lax.rem(chip + step, chips)
        pl.semaphore_signal(
            barrier, inc=1, device_id={"grp": other * 2 + core}, device_id_type=MESH
        )
        return carry

    lax.fori_loop(1, chips, greet_chip, 0)
    pl.semaphore_signal(
        barrier, inc=1, device_id={"grp": chip * 2 + 1 - core}, device_id_type=MESH
    )
    if sectors:
        owner = lax.axis_index("sector")

        def greet_owner(step, carry):
            pl.semaphore_signal(
                barrier,
                inc=1,
                device_id={"sector": lax.rem(owner + step, sectors)},
                device_id_type=MESH,
            )
            return carry

        lax.fori_loop(1, sectors, greet_owner, 0)
        pl.semaphore_wait(barrier, chips + sectors - 1)
    else:
        pl.semaphore_wait(barrier, chips)


def spread(held, chips, chip, core, send_sem, recv_sem, pair_send, pair_recv):
    sibling = {"grp": chip * 2 + 1 - core}
    mine = held.at[chip, core]

    def outgoing(step):
        other = lax.rem(chip + step, chips)
        return send_to(
            mine, mine, send_sem.at[step], recv_sem.at[step], {"grp": other * 2 + core}
        )

    def forward(step):
        source = lax.rem(chip + chips - step, chips)
        block = held.at[source, core]
        return send_to(block, block, pair_send.at[step], pair_recv.at[step], sibling)

    def start(step, carry):
        outgoing(step).start()
        return carry

    def relay(step, carry):
        outgoing(step).wait_recv()
        forward(step).start()
        return carry

    def finish(step, carry):
        outgoing(step).wait_send()
        return carry

    def finish_pair(step, carry):
        forward(step).wait()
        return carry

    lax.fori_loop(1, chips, start, 0)
    forward(0).start()
    lax.fori_loop(1, chips, relay, 0)
    lax.fori_loop(1, chips, finish, 0)
    lax.fori_loop(0, chips, finish_pair, 0)


def gather_kernel(chips, rows_ref, site_ref, env_ref, rows_out, site_out, env_out, *sems):
    position = lax.axis_index("grp")
    chip, core = position // 2, lax.rem(position, 2)
    send_sem, recv_sem, pair_send, pair_recv = sems
    pairs = ((rows_ref, rows_out), (site_ref, site_out), (env_ref, env_out))
    for source, target in pairs:
        target[chip, core] = source[...]
    greet(chips, chip, core)
    sibling = {"grp": chip * 2 + 1 - core}

    def outgoing(item, step):
        other = lax.rem(chip + step, chips)
        mine = pairs[item][1].at[chip, core]
        return send_to(
            mine,
            mine,
            send_sem.at[item, step],
            recv_sem.at[item, step],
            {"grp": other * 2 + core},
        )

    def forward(item, step):
        source = lax.rem(chip + chips - step, chips)
        block = pairs[item][1].at[source, core]
        return send_to(block, block, pair_send.at[item, step], pair_recv.at[item, step], sibling)

    def start(step, carry):
        for item in (1, 2, 0):
            outgoing(item, step).start()
        return carry

    def relay(step, carry):
        for item in (1, 2, 0):
            outgoing(item, step).wait_recv()
            forward(item, step).start()
        return carry

    def finish(step, carry):
        for item in (1, 2, 0):
            outgoing(item, step).wait_send()
        return carry

    def finish_pair(step, carry):
        for item in (1, 2, 0):
            forward(item, step).wait()
        return carry

    lax.fori_loop(1, chips, start, 0)
    for item in (1, 2, 0):
        forward(item, 0).start()
    lax.fori_loop(1, chips, relay, 0)
    lax.fori_loop(1, chips, finish, 0)
    lax.fori_loop(0, chips, finish_pair, 0)


def gather_all(start_vector, site_right, right_env):
    chips = lax.axis_size("grp") // 2
    operands = (start_vector, site_right, right_env)
    return pl.pallas_call(
        functools.partial(gather_kernel, chips),
        out_shape=[jax.ShapeDtypeStruct((chips, 2) + a.shape, a.dtype) for a in operands],
        in_specs=[pl.BlockSpec(memory_space=pltpu.VMEM)] * 3,
        out_specs=[pl.BlockSpec(memory_space=pltpu.VMEM)] * 3,
        scratch_shapes=[pltpu.SemaphoreType.DMA((3, chips))] * 4,
        compiler_params=pltpu.CompilerParams(collective_id=0, has_side_effects=True),
    )(*operands)


def product(dense_ref, mix_ref, vector, part, base):
    tile = 256

    def one_tile(index, carry):
        rows = pl.ds(pl.multiple_of(index * tile, tile), tile)
        total = jnp.zeros((tile, vector.shape[1]), jnp.float32)
        for channel in range(dense_ref.shape[0]):
            mixed = jnp.dot(
                dense_ref[channel, rows, :], vector, preferred_element_type=jnp.float32
            ).astype(jnp.bfloat16)
            total += jnp.dot(mixed, mix_ref[channel], preferred_element_type=jnp.float32)
        split = total.astype(jnp.bfloat16).reshape(tile // (2 * SHARE), 2, SHARE, vector.shape[1])
        chunk = pl.ds(index * (tile // (2 * SHARE)), tile // (2 * SHARE))
        part[base, chunk] = split[:, 0]
        part[base + 1, chunk] = split[:, 1]
        return carry

    lax.fori_loop(0, TPO * TR // tile, one_tile, 0)


def reduce_share(chips, chip, core, part, base, sib, ready, got, sems):
    pair_send, pair_recv, send_sem, recv_sem = sems
    pair = send_to(
        part.at[base + 1 - core],
        sib,
        pair_send,
        pair_recv,
        {"grp": chip * 2 + 1 - core},
    )
    pair.start()
    pair.wait()
    ready[...] = (part[base + core].astype(jnp.float32) + sib[...].astype(jnp.float32)).astype(
        jnp.bfloat16
    )

    def outgoing(step):
        other = lax.rem(chip + step, chips)
        return send_to(
            ready.at[other],
            got.at[step],
            send_sem.at[step],
            recv_sem.at[step],
            {"grp": other * 2 + core},
        )

    def start(step, carry):
        outgoing(step).start()
        return carry

    def collect(step, total):
        outgoing(step).wait_recv()
        return total + got[step].astype(jnp.float32)

    def finish(step, carry):
        outgoing(step).wait_send()
        return carry

    lax.fori_loop(1, chips, start, 0)
    total = lax.fori_loop(1, chips, collect, ready[chip].astype(jnp.float32))
    lax.fori_loop(1, chips, finish, 0)
    return total


def step_kernel(
    chips,
    sectors,
    dense_ref,
    mix_ref,
    start_ref,
    mask_ref,
    first_out,
    second_out,
    part,
    sib_one,
    sib_two,
    ready_one,
    ready_two,
    got_one,
    got_two,
    held,
    norm_mine,
    norm_got,
    pair_sems,
    share_sems,
    spread_sems,
    norm_sems,
):
    position = lax.axis_index("grp")
    owner = lax.axis_index("sector")
    chip, core = position // 2, lax.rem(position, 2)
    rows = TPO * TR
    columns = start_ref.shape[-1]
    greet(chips, chip, core, sectors)
    masked = start_ref[...].reshape(rows, columns) * mask_ref[...].astype(jnp.bfloat16)
    product(dense_ref, mix_ref, masked, part, 0)
    share_mask = mask_ref[pl.ds(pl.multiple_of(position * SHARE, SHARE), SHARE), :]
    total = reduce_share(
        chips,
        chip,
        core,
        part,
        0,
        sib_one,
        ready_one,
        got_one,
        (pair_sems.at[0], pair_sems.at[1], share_sems.at[0], share_sems.at[1]),
    )
    first = (total * share_mask).astype(jnp.bfloat16)
    first_out[...] = first
    held[chip, core] = first
    spread(
        held,
        chips,
        chip,
        core,
        spread_sems.at[0],
        spread_sems.at[1],
        spread_sems.at[2],
        spread_sems.at[3],
    )
    wide = held[...].reshape(rows, columns).astype(jnp.float32)
    squares = jnp.sum((wide * wide).reshape(rows // 8, 8, columns), axis=0)
    norm_mine[...] = sum(squares[:, at : at + 128] for at in range(0, columns, 128))

    def norm_copy(step):
        return send_to(
            norm_mine,
            norm_got.at[step],
            norm_sems.at[0, step],
            norm_sems.at[1, step],
            {"sector": lax.rem(owner + step, sectors)},
        )

    def norm_start(step, carry):
        norm_copy(step).start()
        return carry

    def norm_collect(step, carry):
        norm_copy(step).wait()
        return carry + norm_got[step]

    lax.fori_loop(1, sectors, norm_start, 0)
    product(dense_ref, mix_ref, held[...].reshape(rows, columns), part, 2)
    total = reduce_share(
        chips,
        chip,
        core,
        part,
        2,
        sib_two,
        ready_two,
        got_two,
        (pair_sems.at[2], pair_sems.at[3], share_sems.at[2], share_sems.at[3]),
    )
    sums = lax.fori_loop(1, sectors, norm_collect, norm_mine[...])
    count = float(sectors * rows * columns)
    inverse_norm = lax.rsqrt(jnp.sum(sums, keepdims=True) / count + epsilon)
    second_out[...] = (total * inverse_norm * share_mask).astype(jnp.bfloat16)


def two_products(dense, mixing, owned_rows, owner_mask):
    chips = lax.axis_size("grp") // 2
    sectors = lax.axis_size("sector")
    columns = owned_rows.shape[-1]
    shares = pltpu.VMEM((chips, SHARE, columns), jnp.bfloat16)
    share = jax.ShapeDtypeStruct((SHARE, columns), jnp.bfloat16)
    return pl.pallas_call(
        functools.partial(step_kernel, chips, sectors),
        out_shape=[share, share],
        in_specs=[pl.BlockSpec(memory_space=pltpu.VMEM)] * 4,
        out_specs=[pl.BlockSpec(memory_space=pltpu.VMEM)] * 2,
        scratch_shapes=[
            pltpu.VMEM((4, chips, SHARE, columns), jnp.bfloat16),
            shares,
            shares,
            shares,
            shares,
            shares,
            shares,
            pltpu.VMEM((chips, 2, SHARE, columns), jnp.bfloat16),
            pltpu.VMEM((8, 128), jnp.float32),
            pltpu.VMEM((sectors, 8, 128), jnp.float32),
            pltpu.SemaphoreType.DMA((4,)),
            pltpu.SemaphoreType.DMA((4, chips)),
            pltpu.SemaphoreType.DMA((4, chips)),
            pltpu.SemaphoreType.DMA((2, sectors)),
        ],
        compiler_params=pltpu.CompilerParams(
            collective_id=1, has_side_effects=True, vmem_limit_bytes=40 * 1024 * 1024
        ),
    )(dense, mixing, owned_rows, owner_mask)


def pack_kernel(pick_ref, env_ref, out_ref):
    def one_slot(slot, carry):
        pick = pick_ref[slot]

        @pl.when(pick > 0)
        def _():
            out_ref[slot] = env_ref[pick - 1]

        @pl.when(pick <= 0)
        def _():
            out_ref[slot] = jnp.zeros_like(out_ref[slot])

        return carry

    lax.fori_loop(0, out_ref.shape[0], one_slot, 0)


def pack(pick, blocks):
    return pl.pallas_call(
        pack_kernel,
        out_shape=jax.ShapeDtypeStruct((pick.shape[0], TR, TR), blocks.dtype),
        in_specs=[
            pl.BlockSpec(memory_space=pltpu.SMEM),
            pl.BlockSpec(memory_space=pltpu.VMEM),
        ],
        out_specs=pl.BlockSpec(memory_space=pltpu.VMEM),
    )(pick, blocks)


def assemble_kernel(code_ref, blocks_ref, out_ref, total):
    total[...] = jnp.zeros_like(total)
    channels = out_ref.shape[0]

    def one_slot(slot, carry):
        code = code_ref[slot]
        channel = lax.rem(slot // CAP, channels)

        @pl.when(code > 0)
        def _():
            place = channel * TPO * TPO + code - 1
            total[place] = total[place] + blocks_ref[slot].astype(jnp.float32)

        return carry

    lax.fori_loop(0, blocks_ref.shape[0], one_slot, 0)
    for channel in range(channels):
        for row in range(TPO):
            for col in range(TPO):
                out_ref[channel, row * TR : (row + 1) * TR, col * TR : (col + 1) * TR] = total[
                    (channel * TPO + row) * TPO + col
                ].astype(out_ref.dtype)


def assemble(codes, blocks, channels):
    return pl.pallas_call(
        assemble_kernel,
        out_shape=jax.ShapeDtypeStruct((channels, TPO * TR, TPO * TR), jnp.bfloat16),
        in_specs=[
            pl.BlockSpec(memory_space=pltpu.SMEM),
            pl.BlockSpec(memory_space=pltpu.VMEM),
        ],
        out_specs=pl.BlockSpec(memory_space=pltpu.VMEM),
        scratch_shapes=[pltpu.VMEM((channels * TPO * TPO, TR, TR), jnp.float32)],
    )(codes, blocks)


def mixing_kernel(left_ref, site_ref, env_ref, out_ref, wide):
    group = D1 * WM
    joined = jnp.concatenate(
        [
            jnp.dot(
                left_ref[...],
                site_ref[:, d * group : (d + 1) * group],
                preferred_element_type=jnp.float32,
            )
            for d in range(D1)
        ],
        axis=0,
    ).astype(jnp.bfloat16)
    lanes = D1 * RB
    held = out_ref.shape[0] * D1
    source = lax.broadcasted_iota(jnp.int32, (lanes, D1 * lanes), 0)
    column = lax.broadcasted_iota(jnp.int32, (lanes, D1 * lanes), 1)
    repeat = jnp.where(
        source == (column // lanes) * RB + lax.rem(column, RB), 1.0, 0.0
    ).astype(jnp.bfloat16)
    piece = lax.rem(lax.broadcasted_iota(jnp.int32, (WM, D1 * lanes), 1), lanes) // RB
    for tile in range(RB // D1):
        spread_env = jnp.dot(
            env_ref[:, tile * lanes : (tile + 1) * lanes],
            repeat,
            preferred_element_type=jnp.float32,
        )
        stacked = jnp.concatenate(
            [jnp.where(piece == b, spread_env, 0.0) for b in range(D1)], axis=0
        ).astype(jnp.bfloat16)
        result = jnp.dot(joined, stacked, preferred_element_type=jnp.float32)
        for d in range(D1):
            for a in range(D1):
                at = (d * D1 + a) * held
                for k in range(D1):
                    wide[:, d * RB + tile * D1 + k, a * lanes : (a + 1) * lanes] = result[
                        at : at + held, k * lanes : (k + 1) * lanes
                    ]
    for channel in range(out_ref.shape[0]):
        out_ref[channel] = (
            wide[channel * D1 : (channel + 1) * D1]
            .reshape(out_ref.shape[1], out_ref.shape[2])
            .astype(out_ref.dtype)
        )


def build_mixing(left, site, env, channels):
    columns = PHYS * RB
    return pl.pallas_call(
        mixing_kernel,
        out_shape=jax.ShapeDtypeStruct((channels, columns, columns), jnp.bfloat16),
        in_specs=[pl.BlockSpec(memory_space=pltpu.VMEM)] * 3,
        out_specs=pl.BlockSpec(memory_space=pltpu.VMEM),
        scratch_shapes=[pltpu.VMEM((channels * D1, D1 * RB, columns), jnp.float32)],
    )(left, site, env)


def local(
    start_vector,
    tile_live,
    env_blocks,
    block_owner,
    block_rows,
    block_cols,
    site_left,
    mpo_pattern,
    site_right,
    right_env,
):
    sectors = lax.axis_size("sector")
    channels = env_blocks.shape[0]
    held_blocks = env_blocks.shape[1]
    site_local = (
        site_right.reshape(channels, WM, D1, D1).transpose(0, 3, 2, 1).reshape(channels, WM * PHYS)
    )
    left_site = (
        site_left.reshape(channels, WM, D1, D1) * mpo_pattern.astype(jnp.bfloat16)[:, :, None, None]
    )
    left_rows = left_site.transpose(2, 0, 3, 1).reshape(D1 * channels * D1, WM)
    owned_rows, site_all, env_all = gather_all(start_vector, site_local, right_env)
    mixing = build_mixing(
        left_rows, site_all.reshape(WM, WM * PHYS), env_all.reshape(WM, RB * RB), channels
    )
    owners = block_owner[:, :, 0]
    owner_hot = (owners[:, :, None] == jnp.arange(sectors, dtype=jnp.int32)[None, None, :]).astype(
        jnp.int32
    )
    position = jnp.sum((jnp.cumsum(owner_hot, axis=1) - owner_hot) * owner_hot, axis=2)
    slot_index = owners * CAP + position
    select = slot_index[:, :, None] == jnp.arange(sectors * CAP, dtype=jnp.int32)[None, None, :]
    chosen = select.astype(jnp.int32)

    def by_owner(values):
        return values.reshape(channels, sectors, CAP).transpose(1, 0, 2)

    block_number = jnp.arange(1, 1 + channels * held_blocks, dtype=jnp.int32)
    pick = by_owner(
        jnp.sum(chosen * block_number.reshape(channels, held_blocks)[:, :, None], axis=1)
    )
    slot_codes = by_owner(
        jnp.sum(chosen * (1 + block_rows * TPO + block_cols)[:, :, None], axis=1)
    )
    slots = channels * CAP
    packed = pack(
        pick.reshape(sectors * slots), env_blocks.reshape(channels * held_blocks, TR, TR)
    )
    got_codes = lax.all_to_all(
        slot_codes.reshape(sectors, slots), "sector", split_axis=0, concat_axis=0, tiled=True
    )
    got_blocks = lax.all_to_all(
        packed.reshape(sectors, slots, TR, TR),
        "sector",
        split_axis=0,
        concat_axis=0,
        tiled=True,
    )
    dense = assemble(
        got_codes.reshape(sectors * slots), got_blocks.reshape(sectors * slots, TR, TR), channels
    )
    tile_mask = (jnp.arange(TR, dtype=jnp.int32)[None, :] < tile_live[:, None]).reshape(TPO * TR)
    owner_mask = tile_mask.astype(jnp.float32)[:, None]
    return tuple(two_products(dense, mixing, owned_rows, owner_mask))


def solution(mesh):
    in_specs = (
        P(("sector", "grp"), None),
        P("sector"),
        P("grp", "sector", None, None),
        P("grp", "sector", None),
        P("grp", "sector"),
        P("grp", "sector"),
        P("grp", None),
        P("grp", None),
        P("grp", None),
        P("grp", None),
    )
    out_specs = (P(("sector", "grp"), None), P(("sector", "grp"), None))
    return jax.shard_map(local, mesh=mesh, in_specs=in_specs, out_specs=out_specs, check_vma=False)
```

```python
import functools

import jax
import jax.numpy as jnp
from jax import lax
from jax.experimental import pallas as pl
from jax.experimental.pallas import tpu as pltpu
from jax.sharding import PartitionSpec as P

WM = 64
D1 = 4
RB = 32
TR = 128
TPO = 4
CAP = 2
PHYS = 16


epsilon = 1e-06


MESH = pl.DeviceIdType.MESH
SHARE = 16


def send_to(src, dst, send_sem, recv_sem, target):
    return pltpu.make_async_remote_copy(
        src_ref=src,
        dst_ref=dst,
        send_sem=send_sem,
        recv_sem=recv_sem,
        device_id=target,
        device_id_type=MESH,
    )


def greet(chips, chip, core, sectors=0):
    barrier = pltpu.get_barrier_semaphore()

    def greet_chip(step, carry):
        other = lax.rem(chip + step, chips)
        pl.semaphore_signal(
            barrier, inc=1, device_id={"grp": other * 2 + core}, device_id_type=MESH
        )
        return carry

    lax.fori_loop(1, chips, greet_chip, 0)
    pl.semaphore_signal(
        barrier, inc=1, device_id={"grp": chip * 2 + 1 - core}, device_id_type=MESH
    )
    if sectors:
        owner = lax.axis_index("sector")

        def greet_owner(step, carry):
            pl.semaphore_signal(
                barrier,
                inc=1,
                device_id={"sector": lax.rem(owner + step, sectors)},
                device_id_type=MESH,
            )
            return carry

        lax.fori_loop(1, sectors, greet_owner, 0)
        pl.semaphore_wait(barrier, chips + sectors - 1)
    else:
        pl.semaphore_wait(barrier, chips)


NEAR = 4


def offsets(core):
    return (1, -1, 2 - 4 * core)


def spread(items, chips, chip, core, sems):
    far_count = chips // NEAR
    sibling = {"grp": chip * 2 + 1 - core}
    send_sem, recv_sem, pair_send, pair_recv = sems
    numbers = range(len(items))

    def far(item, step):
        mine = items[item].at[chip, core]
        target = lax.rem(chip + step * NEAR, chips)
        return send_to(
            mine,
            mine,
            send_sem.at[item, step],
            recv_sem.at[item, step],
            {"grp": target * 2 + core},
        )

    def near(item, way, step):
        source = lax.rem(chip + chips - step * NEAR, chips)
        block = items[item].at[source, core]
        target = lax.rem(chip + chips + offsets(core)[way], chips)
        index = (way + 1) * far_count + step
        return send_to(
            block,
            block,
            send_sem.at[item, index],
            recv_sem.at[item, index],
            {"grp": target * 2 + core},
        )

    def forward(item, source, index):
        block = items[item].at[source, core]
        return send_to(
            block, block, pair_send.at[item, index], pair_recv.at[item, index], sibling
        )

    def forward_far(item, step):
        return forward(item, lax.rem(chip + chips - step * NEAR, chips), step)

    def forward_near(item, way, step):
        source = lax.rem(chip + 2 * chips - offsets(core)[way] - step * NEAR, chips)
        return forward(item, source, (way + 1) * far_count + step)

    def far_start(step, carry):
        for item in numbers:
            far(item, step).start()
        return carry

    def far_relay(step, carry):
        for item in numbers:
            far(item, step).wait_recv()
            for way in range(NEAR - 1):
                near(item, way, step).start()
            forward_far(item, step).start()
        return carry

    def near_relay(step, carry):
        for item in numbers:
            for way in range(NEAR - 1):
                near(item, way, step).wait_recv()
                forward_near(item, way, step).start()
        return carry

    def far_finish(step, carry):
        for item in numbers:
            far(item, step).wait_send()
        return carry

    def near_finish(step, carry):
        for item in numbers:
            forward_far(item, step).wait()
            for way in range(NEAR - 1):
                near(item, way, step).wait_send()
                forward_near(item, way, step).wait()
        return carry

    lax.fori_loop(1, far_count, far_start, 0)
    for item in numbers:
        for way in range(NEAR - 1):
            near(item, way, 0).start()
        forward_far(item, 0).start()
    lax.fori_loop(1, far_count, far_relay, 0)
    lax.fori_loop(0, far_count, near_relay, 0)
    lax.fori_loop(1, far_count, far_finish, 0)
    lax.fori_loop(0, far_count, near_finish, 0)


def gather_kernel(
    chips,
    sectors,
    rows_ref,
    site_ref,
    env_ref,
    code_ref,
    rows_out,
    site_out,
    env_out,
    code_out,
    send_sem,
    recv_sem,
    pair_send,
    pair_recv,
    code_sems,
):
    position = lax.axis_index("grp")
    owner = lax.axis_index("sector")
    chip, core = position // 2, lax.rem(position, 2)
    for source, target in ((rows_ref, rows_out), (site_ref, site_out), (env_ref, env_out)):
        target[chip, core] = source[...]
    code_out[owner] = code_ref[owner]
    greet(chips, chip, core, sectors)

    def code_copy(step):
        other = lax.rem(owner + step, sectors)
        return send_to(
            code_ref.at[other],
            code_out.at[owner],
            code_sems.at[0, step],
            code_sems.at[1, step],
            {"sector": other},
        )

    def code_start(step, carry):
        code_copy(step).start()
        return carry

    def code_finish(step, carry):
        code_copy(step).wait()
        return carry

    lax.fori_loop(1, sectors, code_start, 0)
    spread(
        (site_out, env_out, rows_out),
        chips,
        chip,
        core,
        (send_sem, recv_sem, pair_send, pair_recv),
    )
    lax.fori_loop(1, sectors, code_finish, 0)


def gather_all(start_vector, site_right, right_env, codes):
    chips = lax.axis_size("grp") // 2
    sectors = lax.axis_size("sector")
    operands = (start_vector, site_right, right_env)
    return pl.pallas_call(
        functools.partial(gather_kernel, chips, sectors),
        out_shape=[jax.ShapeDtypeStruct((chips, 2) + a.shape, a.dtype) for a in operands]
        + [jax.ShapeDtypeStruct(codes.shape, codes.dtype)],
        in_specs=[pl.BlockSpec(memory_space=pltpu.VMEM)] * 4,
        out_specs=[pl.BlockSpec(memory_space=pltpu.VMEM)] * 4,
        scratch_shapes=[pltpu.SemaphoreType.DMA((3, chips))] * 4
        + [pltpu.SemaphoreType.DMA((2, sectors))],
        compiler_params=pltpu.CompilerParams(collective_id=0, has_side_effects=True),
    )(*operands, codes)


def product(dense_ref, mix_ref, vector, part, base):
    tile = 256

    def one_tile(index, carry):
        rows = pl.ds(pl.multiple_of(index * tile, tile), tile)
        total = jnp.zeros((tile, vector.shape[1]), jnp.float32)
        for channel in range(dense_ref.shape[0]):
            mixed = jnp.dot(
                dense_ref[channel, rows, :], vector, preferred_element_type=jnp.float32
            ).astype(jnp.bfloat16)
            total += jnp.dot(mixed, mix_ref[channel], preferred_element_type=jnp.float32)
        held = tile // (2 * SHARE * NEAR)
        split = total.astype(jnp.bfloat16).reshape(held, NEAR, 2, SHARE, vector.shape[1])
        chunk = pl.ds(index * held, held)
        for kind in range(NEAR):
            part[base, kind, chunk] = split[:, kind, 0]
            part[base + 1, kind, chunk] = split[:, kind, 1]
        return carry

    lax.fori_loop(0, TPO * TR // tile, one_tile, 0)


def reduce_share(chips, chip, core, part, base, sib, ready, near_got, far_ready, far_got, sems):
    pair_sems, near_sems, far_sems = sems
    ways = offsets(core)[::-1]
    far_count = chips // NEAR

    def kind_of(way):
        return lax.rem(chip + chips + ways[way], NEAR) if way < NEAR - 1 else lax.rem(chip, NEAR)

    def pair(way):
        kind = kind_of(way)
        return send_to(
            part.at[base + 1 - core, kind],
            sib.at[kind],
            pair_sems.at[0, way],
            pair_sems.at[1, way],
            {"grp": chip * 2 + 1 - core},
        )

    def near(way):
        target = lax.rem(chip + chips + ways[way], chips)
        return send_to(
            ready.at[kind_of(way)],
            near_got.at[way],
            near_sems.at[0, way],
            near_sems.at[1, way],
            {"grp": target * 2 + core},
        )

    def far(step):
        target = lax.rem(chip + step * NEAR, chips)
        return send_to(
            far_ready.at[target // NEAR],
            far_got.at[step],
            far_sems.at[0, step],
            far_sems.at[1, step],
            {"grp": target * 2 + core},
        )

    for way in range(NEAR):
        pair(way).start()
    for way in range(NEAR - 1):
        pair(way).wait_recv()
        kind = kind_of(way)
        ready[kind] = (
            part[base + core, kind].astype(jnp.float32) + sib[kind].astype(jnp.float32)
        ).astype(jnp.bfloat16)
        near(way).start()
    pair(NEAR - 1).wait_recv()
    kind = kind_of(NEAR - 1)
    total = part[base + core, kind].astype(jnp.float32) + sib[kind].astype(jnp.float32)
    for way in range(NEAR - 1):
        near(way).wait_recv()
        total += near_got[way].astype(jnp.float32)
    far_ready[...] = total.astype(jnp.bfloat16)
    for step in range(1, far_count):
        far(step).start()
    share = far_ready[chip // NEAR].astype(jnp.float32)
    for step in range(1, far_count):
        far(step).wait_recv()
        share += far_got[step].astype(jnp.float32)
    for way in range(NEAR):
        pair(way).wait_send()
    for way in range(NEAR - 1):
        near(way).wait_send()
    for step in range(1, far_count):
        far(step).wait_send()
    return share


def step_kernel(
    chips,
    sectors,
    dense_ref,
    mix_ref,
    start_ref,
    mask_ref,
    first_out,
    second_out,
    part,
    sib,
    ready,
    near_got,
    far_ready,
    far_got,
    held,
    norm_mine,
    norm_got,
    pair_sems,
    near_sems,
    far_sems,
    spread_sems,
    norm_sems,
):
    position = lax.axis_index("grp")
    owner = lax.axis_index("sector")
    chip, core = position // 2, lax.rem(position, 2)
    rows = TPO * TR
    columns = start_ref.shape[-1]
    greet(chips, chip, core, sectors)
    masked = start_ref[...].reshape(rows, columns) * mask_ref[...].astype(jnp.bfloat16)
    product(dense_ref, mix_ref, masked, part, 0)
    share_mask = mask_ref[pl.ds(pl.multiple_of(position * SHARE, SHARE), SHARE), :]
    total = reduce_share(
        chips,
        chip,
        core,
        part,
        0,
        sib.at[0],
        ready.at[0],
        near_got.at[0],
        far_ready.at[0],
        far_got.at[0],
        (pair_sems.at[0], near_sems.at[0], far_sems.at[0]),
    )
    first = (total * share_mask).astype(jnp.bfloat16)
    first_out[...] = first
    held[chip, core] = first
    spread((held,), chips, chip, core, [spread_sems.at[at] for at in range(4)])
    wide = held[...].reshape(rows, columns).astype(jnp.float32)
    squares = jnp.sum((wide * wide).reshape(rows // 8, 8, columns), axis=0)
    norm_mine[...] = sum(squares[:, at : at + 128] for at in range(0, columns, 128))

    def norm_copy(step):
        return send_to(
            norm_mine,
            norm_got.at[step],
            norm_sems.at[0, step],
            norm_sems.at[1, step],
            {"sector": lax.rem(owner + step, sectors)},
        )

    def norm_start(step, carry):
        norm_copy(step).start()
        return carry

    def norm_collect(step, carry):
        norm_copy(step).wait()
        return carry + norm_got[step]

    lax.fori_loop(1, sectors, norm_start, 0)
    product(dense_ref, mix_ref, held[...].reshape(rows, columns), part, 2)
    total = reduce_share(
        chips,
        chip,
        core,
        part,
        2,
        sib.at[1],
        ready.at[1],
        near_got.at[1],
        far_ready.at[1],
        far_got.at[1],
        (pair_sems.at[1], near_sems.at[1], far_sems.at[1]),
    )
    sums = lax.fori_loop(1, sectors, norm_collect, norm_mine[...])
    count = float(sectors * rows * columns)
    inverse_norm = lax.rsqrt(jnp.sum(sums, keepdims=True) / count + epsilon)
    second_out[...] = (total * inverse_norm * share_mask).astype(jnp.bfloat16)


def two_products(dense, mixing, owned_rows, owner_mask):
    chips = lax.axis_size("grp") // 2
    sectors = lax.axis_size("sector")
    columns = owned_rows.shape[-1]
    shares = (chips // NEAR, SHARE, columns)
    share = jax.ShapeDtypeStruct((SHARE, columns), jnp.bfloat16)
    return pl.pallas_call(
        functools.partial(step_kernel, chips, sectors),
        out_shape=[share, share],
        in_specs=[pl.BlockSpec(memory_space=pltpu.VMEM)] * 4,
        out_specs=[pl.BlockSpec(memory_space=pltpu.VMEM)] * 2,
        scratch_shapes=[
            pltpu.VMEM((4, NEAR) + shares, jnp.bfloat16),
            pltpu.VMEM((2, NEAR) + shares, jnp.bfloat16),
            pltpu.VMEM((2, NEAR) + shares, jnp.bfloat16),
            pltpu.VMEM((2, NEAR - 1) + shares, jnp.bfloat16),
            pltpu.VMEM((2,) + shares, jnp.bfloat16),
            pltpu.VMEM((2,) + shares, jnp.bfloat16),
            pltpu.VMEM((chips, 2, SHARE, columns), jnp.bfloat16),
            pltpu.VMEM((8, 128), jnp.float32),
            pltpu.VMEM((sectors, 8, 128), jnp.float32),
            pltpu.SemaphoreType.DMA((2, 2, NEAR)),
            pltpu.SemaphoreType.DMA((2, 2, NEAR)),
            pltpu.SemaphoreType.DMA((2, 2, chips // NEAR)),
            pltpu.SemaphoreType.DMA((4, 1, chips)),
            pltpu.SemaphoreType.DMA((2, sectors)),
        ],
        compiler_params=pltpu.CompilerParams(
            collective_id=1, has_side_effects=True, vmem_limit_bytes=40 * 1024 * 1024
        ),
    )(dense, mixing, owned_rows, owner_mask)


def pack_kernel(pick_ref, env_ref, out_ref):
    def one_slot(slot, carry):
        pick = pick_ref[slot]

        @pl.when(pick > 0)
        def _():
            out_ref[slot] = env_ref[pick - 1]

        @pl.when(pick <= 0)
        def _():
            out_ref[slot] = jnp.zeros_like(out_ref[slot])

        return carry

    lax.fori_loop(0, out_ref.shape[0], one_slot, 0)


def pack(pick, blocks):
    return pl.pallas_call(
        pack_kernel,
        out_shape=jax.ShapeDtypeStruct((pick.shape[0], TR, TR), blocks.dtype),
        in_specs=[
            pl.BlockSpec(memory_space=pltpu.SMEM),
            pl.BlockSpec(memory_space=pltpu.VMEM),
        ],
        out_specs=pl.BlockSpec(memory_space=pltpu.VMEM),
    )(pick, blocks)


def assemble_kernel(code_ref, blocks_ref, out_ref, total):
    total[...] = jnp.zeros_like(total)
    channels = out_ref.shape[0]

    def one_slot(slot, carry):
        code = code_ref[slot]
        channel = lax.rem(slot // CAP, channels)

        @pl.when(code > 0)
        def _():
            place = channel * TPO * TPO + code - 1
            total[place] = total[place] + blocks_ref[slot].astype(jnp.float32)

        return carry

    lax.fori_loop(0, blocks_ref.shape[0], one_slot, 0)
    for channel in range(channels):
        for row in range(TPO):
            for col in range(TPO):
                out_ref[channel, row * TR : (row + 1) * TR, col * TR : (col + 1) * TR] = total[
                    (channel * TPO + row) * TPO + col
                ].astype(out_ref.dtype)


def assemble(codes, blocks, channels):
    return pl.pallas_call(
        assemble_kernel,
        out_shape=jax.ShapeDtypeStruct((channels, TPO * TR, TPO * TR), jnp.bfloat16),
        in_specs=[
            pl.BlockSpec(memory_space=pltpu.SMEM),
            pl.BlockSpec(memory_space=pltpu.VMEM),
        ],
        out_specs=pl.BlockSpec(memory_space=pltpu.VMEM),
        scratch_shapes=[pltpu.VMEM((channels * TPO * TPO, TR, TR), jnp.float32)],
    )(codes, blocks)


def mixing_kernel(left_ref, site_ref, env_ref, out_ref, wide):
    group = D1 * WM
    joined = jnp.concatenate(
        [
            jnp.dot(
                left_ref[...],
                site_ref[:, d * group : (d + 1) * group],
                preferred_element_type=jnp.float32,
            )
            for d in range(D1)
        ],
        axis=0,
    ).astype(jnp.bfloat16)
    lanes = D1 * RB
    held = out_ref.shape[0] * D1
    source = lax.broadcasted_iota(jnp.int32, (lanes, D1 * lanes), 0)
    column = lax.broadcasted_iota(jnp.int32, (lanes, D1 * lanes), 1)
    repeat = jnp.where(
        source == (column // lanes) * RB + lax.rem(column, RB), 1.0, 0.0
    ).astype(jnp.bfloat16)
    piece = lax.rem(lax.broadcasted_iota(jnp.int32, (WM, D1 * lanes), 1), lanes) // RB
    for tile in range(RB // D1):
        spread_env = jnp.dot(
            env_ref[:, tile * lanes : (tile + 1) * lanes],
            repeat,
            preferred_element_type=jnp.float32,
        )
        stacked = jnp.concatenate(
            [jnp.where(piece == b, spread_env, 0.0) for b in range(D1)], axis=0
        ).astype(jnp.bfloat16)
        result = jnp.dot(joined, stacked, preferred_element_type=jnp.float32)
        for d in range(D1):
            for a in range(D1):
                at = (d * D1 + a) * held
                for k in range(D1):
                    wide[:, d * RB + tile * D1 + k, a * lanes : (a + 1) * lanes] = result[
                        at : at + held, k * lanes : (k + 1) * lanes
                    ]
    for channel in range(out_ref.shape[0]):
        out_ref[channel] = (
            wide[channel * D1 : (channel + 1) * D1]
            .reshape(out_ref.shape[1], out_ref.shape[2])
            .astype(out_ref.dtype)
        )


def build_mixing(left, site, env, channels):
    columns = PHYS * RB
    return pl.pallas_call(
        mixing_kernel,
        out_shape=jax.ShapeDtypeStruct((channels, columns, columns), jnp.bfloat16),
        in_specs=[pl.BlockSpec(memory_space=pltpu.VMEM)] * 3,
        out_specs=pl.BlockSpec(memory_space=pltpu.VMEM),
        scratch_shapes=[pltpu.VMEM((channels * D1, D1 * RB, columns), jnp.float32)],
    )(left, site, env)


def local(
    start_vector,
    tile_live,
    env_blocks,
    block_owner,
    block_rows,
    block_cols,
    site_left,
    mpo_pattern,
    site_right,
    right_env,
):
    sectors = lax.axis_size("sector")
    channels = env_blocks.shape[0]
    held_blocks = env_blocks.shape[1]
    site_local = (
        site_right.reshape(channels, WM, D1, D1).transpose(0, 3, 2, 1).reshape(channels, WM * PHYS)
    )
    left_site = (
        site_left.reshape(channels, WM, D1, D1) * mpo_pattern.astype(jnp.bfloat16)[:, :, None, None]
    )
    left_rows = left_site.transpose(2, 0, 3, 1).reshape(D1 * channels * D1, WM)
    owners = block_owner[:, :, 0]
    owner_hot = (owners[:, :, None] == jnp.arange(sectors, dtype=jnp.int32)[None, None, :]).astype(
        jnp.int32
    )
    position = jnp.sum((jnp.cumsum(owner_hot, axis=1) - owner_hot) * owner_hot, axis=2)
    slot_index = owners * CAP + position
    select = slot_index[:, :, None] == jnp.arange(sectors * CAP, dtype=jnp.int32)[None, None, :]
    chosen = select.astype(jnp.int32)

    def by_owner(values):
        return values.reshape(channels, sectors, CAP).transpose(1, 0, 2)

    block_number = jnp.arange(1, 1 + channels * held_blocks, dtype=jnp.int32)
    pick = by_owner(
        jnp.sum(chosen * block_number.reshape(channels, held_blocks)[:, :, None], axis=1)
    )
    slot_codes = by_owner(
        jnp.sum(chosen * (1 + block_rows * TPO + block_cols)[:, :, None], axis=1)
    )
    slots = channels * CAP
    packed = pack(
        pick.reshape(sectors * slots), env_blocks.reshape(channels * held_blocks, TR, TR)
    )
    got_blocks = lax.all_to_all(
        packed.reshape(sectors, slots, TR, TR),
        "sector",
        split_axis=0,
        concat_axis=0,
        tiled=True,
    )
    owned_rows, site_all, env_all, got_codes = gather_all(
        start_vector, site_local, right_env, slot_codes.reshape(sectors, 1, slots)
    )
    mixing = build_mixing(
        left_rows, site_all.reshape(WM, WM * PHYS), env_all.reshape(WM, RB * RB), channels
    )
    dense = assemble(
        got_codes.reshape(sectors * slots), got_blocks.reshape(sectors * slots, TR, TR), channels
    )
    tile_mask = (jnp.arange(TR, dtype=jnp.int32)[None, :] < tile_live[:, None]).reshape(TPO * TR)
    owner_mask = tile_mask.astype(jnp.float32)[:, None]
    return tuple(two_products(dense, mixing, owned_rows, owner_mask))


def solution(mesh):
    in_specs = (
        P(("sector", "grp"), None),
        P("sector"),
        P("grp", "sector", None, None),
        P("grp", "sector", None),
        P("grp", "sector"),
        P("grp", "sector"),
        P("grp", None),
        P("grp", None),
        P("grp", None),
        P("grp", None),
    )
    out_specs = (P(("sector", "grp"), None), P(("sector", "grp"), None))
    return jax.shard_map(local, mesh=mesh, in_specs=in_specs, out_specs=out_specs, check_vma=False)
```

```python
import functools

import jax
import jax.numpy as jnp
from jax import lax
from jax.experimental import pallas as pl
from jax.experimental.pallas import tpu as pltpu
from jax.sharding import PartitionSpec as P

WM = 64
D1 = 4
RB = 32
TR = 128
TPO = 4
CAP = 2
PHYS = 16


epsilon = 1e-06


MESH = pl.DeviceIdType.MESH
SHARE = 16


def send_to(src, dst, send_sem, recv_sem, target):
    return pltpu.make_async_remote_copy(
        src_ref=src,
        dst_ref=dst,
        send_sem=send_sem,
        recv_sem=recv_sem,
        device_id=target,
        device_id_type=MESH,
    )


def greet(chips, chip, core, sectors):
    barrier = pltpu.get_barrier_semaphore()

    def greet_chip(step, carry):
        other = lax.rem(chip + step, chips)
        pl.semaphore_signal(
            barrier, inc=1, device_id={"grp": other * 2 + core}, device_id_type=MESH
        )
        return carry

    lax.fori_loop(1, chips, greet_chip, 0)
    pl.semaphore_signal(
        barrier, inc=1, device_id={"grp": chip * 2 + 1 - core}, device_id_type=MESH
    )
    owner = lax.axis_index("sector")

    def greet_owner(step, carry):
        pl.semaphore_signal(
            barrier,
            inc=1,
            device_id={"sector": lax.rem(owner + step, sectors)},
            device_id_type=MESH,
        )
        return carry

    lax.fori_loop(1, sectors, greet_owner, 0)


def await_greetings(chips, sectors):
    pl.semaphore_wait(pltpu.get_barrier_semaphore(), chips + sectors - 1)


NEAR = 4


def offsets(core):
    return (1, -1, 2 - 4 * core)


def spread(items, chips, chip, core, sems):
    far_count = chips // NEAR
    sibling = {"grp": chip * 2 + 1 - core}
    send_sem, recv_sem, pair_send, pair_recv = sems
    numbers = range(len(items))

    def far(item, step):
        mine = items[item].at[chip, core]
        target = lax.rem(chip + step * NEAR, chips)
        return send_to(
            mine,
            mine,
            send_sem.at[item, step],
            recv_sem.at[item, step],
            {"grp": target * 2 + core},
        )

    def near(item, way, step):
        source = lax.rem(chip + chips - step * NEAR, chips)
        block = items[item].at[source, core]
        target = lax.rem(chip + chips + offsets(core)[way], chips)
        index = (way + 1) * far_count + step
        return send_to(
            block,
            block,
            send_sem.at[item, index],
            recv_sem.at[item, index],
            {"grp": target * 2 + core},
        )

    def forward(item, source, index):
        block = items[item].at[source, core]
        return send_to(
            block, block, pair_send.at[item, index], pair_recv.at[item, index], sibling
        )

    def forward_far(item, step):
        return forward(item, lax.rem(chip + chips - step * NEAR, chips), step)

    def forward_near(item, way, step):
        source = lax.rem(chip + 2 * chips - offsets(core)[way] - step * NEAR, chips)
        return forward(item, source, (way + 1) * far_count + step)

    def far_start(step, carry):
        for item in numbers:
            far(item, step).start()
        return carry

    def far_relay(step, carry):
        for item in numbers:
            far(item, step).wait_recv()
            for way in range(NEAR - 1):
                near(item, way, step).start()
            forward_far(item, step).start()
        return carry

    def near_relay(step, carry):
        for item in numbers:
            for way in range(NEAR - 1):
                near(item, way, step).wait_recv()
                forward_near(item, way, step).start()
        return carry

    def far_finish(step, carry):
        for item in numbers:
            far(item, step).wait_send()
        return carry

    def near_finish(step, carry):
        for item in numbers:
            forward_far(item, step).wait()
            for way in range(NEAR - 1):
                near(item, way, step).wait_send()
                forward_near(item, way, step).wait()
        return carry

    lax.fori_loop(1, far_count, far_start, 0)
    for item in numbers:
        for way in range(NEAR - 1):
            near(item, way, 0).start()
        forward_far(item, 0).start()
    lax.fori_loop(1, far_count, far_relay, 0)
    lax.fori_loop(0, far_count, near_relay, 0)
    lax.fori_loop(1, far_count, far_finish, 0)
    lax.fori_loop(0, far_count, near_finish, 0)


def gather_kernel(
    chips,
    sectors,
    rows_ref,
    site_ref,
    env_ref,
    code_ref,
    rows_out,
    site_out,
    env_out,
    code_out,
    send_sem,
    recv_sem,
    pair_send,
    pair_recv,
    code_sems,
):
    position = lax.axis_index("grp")
    owner = lax.axis_index("sector")
    chip, core = position // 2, lax.rem(position, 2)
    greet(chips, chip, core, sectors)
    for source, target in ((rows_ref, rows_out), (site_ref, site_out), (env_ref, env_out)):
        target[chip, core] = source[...]
    code_out[owner] = code_ref[owner]
    await_greetings(chips, sectors)

    def code_copy(step):
        other = lax.rem(owner + step, sectors)
        return send_to(
            code_ref.at[other],
            code_out.at[owner],
            code_sems.at[0, step],
            code_sems.at[1, step],
            {"sector": other},
        )

    def code_start(step, carry):
        code_copy(step).start()
        return carry

    def code_finish(step, carry):
        code_copy(step).wait()
        return carry

    lax.fori_loop(1, sectors, code_start, 0)
    spread(
        (site_out, env_out, rows_out),
        chips,
        chip,
        core,
        (send_sem, recv_sem, pair_send, pair_recv),
    )
    lax.fori_loop(1, sectors, code_finish, 0)


def gather_all(start_vector, site_right, right_env, codes):
    chips = lax.axis_size("grp") // 2
    sectors = lax.axis_size("sector")
    operands = (start_vector, site_right, right_env)
    return pl.pallas_call(
        functools.partial(gather_kernel, chips, sectors),
        out_shape=[jax.ShapeDtypeStruct((chips, 2) + a.shape, a.dtype) for a in operands]
        + [jax.ShapeDtypeStruct(codes.shape, codes.dtype)],
        in_specs=[pl.BlockSpec(memory_space=pltpu.VMEM)] * 4,
        out_specs=[pl.BlockSpec(memory_space=pltpu.VMEM)] * 4,
        scratch_shapes=[pltpu.SemaphoreType.DMA((3, chips))] * 4
        + [pltpu.SemaphoreType.DMA((2, sectors))],
        compiler_params=pltpu.CompilerParams(collective_id=0, has_side_effects=True),
    )(*operands, codes)


def product(dense_ref, mix_ref, vector, part, base):
    tile = 256

    def one_tile(index, carry):
        rows = pl.ds(pl.multiple_of(index * tile, tile), tile)
        total = jnp.zeros((tile, vector.shape[1]), jnp.float32)
        for channel in range(dense_ref.shape[0]):
            mixed = jnp.dot(
                dense_ref[channel, rows, :], vector, preferred_element_type=jnp.float32
            ).astype(jnp.bfloat16)
            total += jnp.dot(mixed, mix_ref[channel], preferred_element_type=jnp.float32)
        held = tile // (2 * SHARE * NEAR)
        split = total.astype(jnp.bfloat16).reshape(held, NEAR, 2, SHARE, vector.shape[1])
        chunk = pl.ds(index * held, held)
        for kind in range(NEAR):
            part[base, kind, chunk] = split[:, kind, 0]
            part[base + 1, kind, chunk] = split[:, kind, 1]
        return carry

    lax.fori_loop(0, TPO * TR // tile, one_tile, 0)


def reduce_share(chips, chip, core, part, base, sib, ready, near_got, far_ready, far_got, sems):
    pair_sems, near_sems, far_sems = sems
    ways = offsets(core)[::-1]
    far_count = chips // NEAR

    def kind_of(way):
        return lax.rem(chip + chips + ways[way], NEAR) if way < NEAR - 1 else lax.rem(chip, NEAR)

    def pair(way):
        kind = kind_of(way)
        return send_to(
            part.at[base + 1 - core, kind],
            sib.at[kind],
            pair_sems.at[0, way],
            pair_sems.at[1, way],
            {"grp": chip * 2 + 1 - core},
        )

    def near(way):
        target = lax.rem(chip + chips + ways[way], chips)
        return send_to(
            ready.at[kind_of(way)],
            near_got.at[way],
            near_sems.at[0, way],
            near_sems.at[1, way],
            {"grp": target * 2 + core},
        )

    def far(step):
        target = lax.rem(chip + step * NEAR, chips)
        return send_to(
            far_ready.at[target // NEAR],
            far_got.at[step],
            far_sems.at[0, step],
            far_sems.at[1, step],
            {"grp": target * 2 + core},
        )

    for way in range(NEAR):
        pair(way).start()
    for way in range(NEAR - 1):
        pair(way).wait_recv()
        kind = kind_of(way)
        ready[kind] = (
            part[base + core, kind].astype(jnp.float32) + sib[kind].astype(jnp.float32)
        ).astype(jnp.bfloat16)
        near(way).start()
    pair(NEAR - 1).wait_recv()
    kind = kind_of(NEAR - 1)
    total = part[base + core, kind].astype(jnp.float32) + sib[kind].astype(jnp.float32)
    for way in range(NEAR - 1):
        near(way).wait_recv()
        total += near_got[way].astype(jnp.float32)
    far_ready[...] = total.astype(jnp.bfloat16)
    for step in range(1, far_count):
        far(step).start()
    share = far_ready[chip // NEAR].astype(jnp.float32)
    for step in range(1, far_count):
        far(step).wait_recv()
        share += far_got[step].astype(jnp.float32)
    for way in range(NEAR):
        pair(way).wait_send()
    for way in range(NEAR - 1):
        near(way).wait_send()
    for step in range(1, far_count):
        far(step).wait_send()
    return share


def step_kernel(
    chips,
    sectors,
    dense_ref,
    left_ref,
    site_ref,
    env_ref,
    start_ref,
    mask_ref,
    first_out,
    second_out,
    mix_ref,
    wide_mix,
    part,
    sib,
    ready,
    near_got,
    far_ready,
    far_got,
    held,
    norm_mine,
    norm_got,
    pair_sems,
    near_sems,
    far_sems,
    spread_sems,
    norm_sems,
):
    position = lax.axis_index("grp")
    owner = lax.axis_index("sector")
    chip, core = position // 2, lax.rem(position, 2)
    rows = TPO * TR
    columns = start_ref.shape[-1]
    greet(chips, chip, core, sectors)
    fill_mixing(left_ref, site_ref, env_ref, mix_ref, wide_mix)
    masked = start_ref[...].reshape(rows, columns) * mask_ref[...].astype(jnp.bfloat16)
    product(dense_ref, mix_ref, masked, part, 0)
    await_greetings(chips, sectors)
    share_mask = mask_ref[pl.ds(pl.multiple_of(position * SHARE, SHARE), SHARE), :]
    total = reduce_share(
        chips,
        chip,
        core,
        part,
        0,
        sib.at[0],
        ready.at[0],
        near_got.at[0],
        far_ready.at[0],
        far_got.at[0],
        (pair_sems.at[0], near_sems.at[0], far_sems.at[0]),
    )
    first = (total * share_mask).astype(jnp.bfloat16)
    first_out[...] = first
    held[chip, core] = first
    spread((held,), chips, chip, core, [spread_sems.at[at] for at in range(4)])
    wide = held[...].reshape(rows, columns).astype(jnp.float32)
    squares = jnp.sum((wide * wide).reshape(rows // 8, 8, columns), axis=0)
    norm_mine[...] = sum(squares[:, at : at + 128] for at in range(0, columns, 128))

    def norm_copy(step):
        return send_to(
            norm_mine,
            norm_got.at[step],
            norm_sems.at[0, step],
            norm_sems.at[1, step],
            {"sector": lax.rem(owner + step, sectors)},
        )

    def norm_start(step, carry):
        norm_copy(step).start()
        return carry

    def norm_collect(step, carry):
        norm_copy(step).wait()
        return carry + norm_got[step]

    lax.fori_loop(1, sectors, norm_start, 0)
    product(dense_ref, mix_ref, held[...].reshape(rows, columns), part, 2)
    total = reduce_share(
        chips,
        chip,
        core,
        part,
        2,
        sib.at[1],
        ready.at[1],
        near_got.at[1],
        far_ready.at[1],
        far_got.at[1],
        (pair_sems.at[1], near_sems.at[1], far_sems.at[1]),
    )
    sums = lax.fori_loop(1, sectors, norm_collect, norm_mine[...])
    count = float(sectors * rows * columns)
    inverse_norm = lax.rsqrt(jnp.sum(sums, keepdims=True) / count + epsilon)
    second_out[...] = (total * inverse_norm * share_mask).astype(jnp.bfloat16)


def two_products(dense, left, site, env, owned_rows, owner_mask):
    chips = lax.axis_size("grp") // 2
    sectors = lax.axis_size("sector")
    columns = owned_rows.shape[-1]
    shares = (chips // NEAR, SHARE, columns)
    share = jax.ShapeDtypeStruct((SHARE, columns), jnp.bfloat16)
    return pl.pallas_call(
        functools.partial(step_kernel, chips, sectors),
        out_shape=[share, share],
        in_specs=[pl.BlockSpec(memory_space=pltpu.VMEM)] * 6,
        out_specs=[pl.BlockSpec(memory_space=pltpu.VMEM)] * 2,
        scratch_shapes=[
            pltpu.VMEM(dense.shape, jnp.bfloat16),
            pltpu.VMEM((dense.shape[0] * D1, D1 * RB, columns), jnp.float32),
            pltpu.VMEM((4, NEAR) + shares, jnp.bfloat16),
            pltpu.VMEM((2, NEAR) + shares, jnp.bfloat16),
            pltpu.VMEM((2, NEAR) + shares, jnp.bfloat16),
            pltpu.VMEM((2, NEAR - 1) + shares, jnp.bfloat16),
            pltpu.VMEM((2,) + shares, jnp.bfloat16),
            pltpu.VMEM((2,) + shares, jnp.bfloat16),
            pltpu.VMEM((chips, 2, SHARE, columns), jnp.bfloat16),
            pltpu.VMEM((8, 128), jnp.float32),
            pltpu.VMEM((sectors, 8, 128), jnp.float32),
            pltpu.SemaphoreType.DMA((2, 2, NEAR)),
            pltpu.SemaphoreType.DMA((2, 2, NEAR)),
            pltpu.SemaphoreType.DMA((2, 2, chips // NEAR)),
            pltpu.SemaphoreType.DMA((4, 1, chips)),
            pltpu.SemaphoreType.DMA((2, sectors)),
        ],
        compiler_params=pltpu.CompilerParams(
            collective_id=1, has_side_effects=True, vmem_limit_bytes=40 * 1024 * 1024
        ),
    )(dense, left, site, env, owned_rows, owner_mask)


def pack_kernel(pick_ref, env_ref, out_ref):
    def one_slot(slot, carry):
        pick = pick_ref[slot]

        @pl.when(pick > 0)
        def _():
            out_ref[slot] = env_ref[pick - 1]

        @pl.when(pick <= 0)
        def _():
            out_ref[slot] = jnp.zeros_like(out_ref[slot])

        return carry

    lax.fori_loop(0, out_ref.shape[0], one_slot, 0)


def pack(pick, blocks):
    return pl.pallas_call(
        pack_kernel,
        out_shape=jax.ShapeDtypeStruct((pick.shape[0], TR, TR), blocks.dtype),
        in_specs=[
            pl.BlockSpec(memory_space=pltpu.SMEM),
            pl.BlockSpec(memory_space=pltpu.VMEM),
        ],
        out_specs=pl.BlockSpec(memory_space=pltpu.VMEM),
    )(pick, blocks)


def assemble_kernel(code_ref, blocks_ref, out_ref, total):
    total[...] = jnp.zeros_like(total)
    channels = out_ref.shape[0]

    def one_slot(slot, carry):
        code = code_ref[slot]
        channel = lax.rem(slot // CAP, channels)

        @pl.when(code > 0)
        def _():
            place = channel * TPO * TPO + code - 1
            total[place] = total[place] + blocks_ref[slot].astype(jnp.float32)

        return carry

    lax.fori_loop(0, blocks_ref.shape[0], one_slot, 0)
    for channel in range(channels):
        for row in range(TPO):
            for col in range(TPO):
                out_ref[channel, row * TR : (row + 1) * TR, col * TR : (col + 1) * TR] = total[
                    (channel * TPO + row) * TPO + col
                ].astype(out_ref.dtype)


def assemble(codes, blocks, channels):
    return pl.pallas_call(
        assemble_kernel,
        out_shape=jax.ShapeDtypeStruct((channels, TPO * TR, TPO * TR), jnp.bfloat16),
        in_specs=[
            pl.BlockSpec(memory_space=pltpu.SMEM),
            pl.BlockSpec(memory_space=pltpu.VMEM),
        ],
        out_specs=pl.BlockSpec(memory_space=pltpu.VMEM),
        scratch_shapes=[pltpu.VMEM((channels * TPO * TPO, TR, TR), jnp.float32)],
    )(codes, blocks)


def fill_mixing(left_ref, site_ref, env_ref, out_ref, wide):
    group = D1 * WM
    joined = jnp.concatenate(
        [
            jnp.dot(
                left_ref[...],
                site_ref[:, d * group : (d + 1) * group],
                preferred_element_type=jnp.float32,
            )
            for d in range(D1)
        ],
        axis=0,
    ).astype(jnp.bfloat16)
    lanes = D1 * RB
    held = out_ref.shape[0] * D1
    source = lax.broadcasted_iota(jnp.int32, (lanes, D1 * lanes), 0)
    column = lax.broadcasted_iota(jnp.int32, (lanes, D1 * lanes), 1)
    repeat = jnp.where(
        source == (column // lanes) * RB + lax.rem(column, RB), 1.0, 0.0
    ).astype(jnp.bfloat16)
    piece = lax.rem(lax.broadcasted_iota(jnp.int32, (WM, D1 * lanes), 1), lanes) // RB
    for tile in range(RB // D1):
        spread_env = jnp.dot(
            env_ref[:, tile * lanes : (tile + 1) * lanes],
            repeat,
            preferred_element_type=jnp.float32,
        )
        stacked = jnp.concatenate(
            [jnp.where(piece == b, spread_env, 0.0) for b in range(D1)], axis=0
        ).astype(jnp.bfloat16)
        result = jnp.dot(joined, stacked, preferred_element_type=jnp.float32)
        for d in range(D1):
            for a in range(D1):
                at = (d * D1 + a) * held
                for k in range(D1):
                    wide[:, d * RB + tile * D1 + k, a * lanes : (a + 1) * lanes] = result[
                        at : at + held, k * lanes : (k + 1) * lanes
                    ]
    for channel in range(out_ref.shape[0]):
        out_ref[channel] = (
            wide[channel * D1 : (channel + 1) * D1]
            .reshape(out_ref.shape[1], out_ref.shape[2])
            .astype(out_ref.dtype)
        )


def local(
    start_vector,
    tile_live,
    env_blocks,
    block_owner,
    block_rows,
    block_cols,
    site_left,
    mpo_pattern,
    site_right,
    right_env,
):
    sectors = lax.axis_size("sector")
    channels = env_blocks.shape[0]
    held_blocks = env_blocks.shape[1]
    site_local = (
        site_right.reshape(channels, WM, D1, D1).transpose(0, 3, 2, 1).reshape(channels, WM * PHYS)
    )
    left_site = (
        site_left.reshape(channels, WM, D1, D1) * mpo_pattern.astype(jnp.bfloat16)[:, :, None, None]
    )
    left_rows = left_site.transpose(2, 0, 3, 1).reshape(D1 * channels * D1, WM)
    owners = block_owner[:, :, 0]
    owner_hot = (owners[:, :, None] == jnp.arange(sectors, dtype=jnp.int32)[None, None, :]).astype(
        jnp.int32
    )
    position = jnp.sum((jnp.cumsum(owner_hot, axis=1) - owner_hot) * owner_hot, axis=2)
    slot_index = owners * CAP + position
    select = slot_index[:, :, None] == jnp.arange(sectors * CAP, dtype=jnp.int32)[None, None, :]
    chosen = select.astype(jnp.int32)

    def by_owner(values):
        return values.reshape(channels, sectors, CAP).transpose(1, 0, 2)

    block_number = jnp.arange(1, 1 + channels * held_blocks, dtype=jnp.int32)
    pick = by_owner(
        jnp.sum(chosen * block_number.reshape(channels, held_blocks)[:, :, None], axis=1)
    )
    slot_codes = by_owner(
        jnp.sum(chosen * (1 + block_rows * TPO + block_cols)[:, :, None], axis=1)
    )
    slots = channels * CAP
    packed = pack(
        pick.reshape(sectors * slots), env_blocks.reshape(channels * held_blocks, TR, TR)
    )
    got_blocks = lax.all_to_all(
        packed.reshape(sectors, slots, TR, TR),
        "sector",
        split_axis=0,
        concat_axis=0,
        tiled=True,
    )
    owned_rows, site_all, env_all, got_codes = gather_all(
        start_vector, site_local, right_env, slot_codes.reshape(sectors, 1, slots)
    )
    dense = assemble(
        got_codes.reshape(sectors * slots), got_blocks.reshape(sectors * slots, TR, TR), channels
    )
    tile_mask = (jnp.arange(TR, dtype=jnp.int32)[None, :] < tile_live[:, None]).reshape(TPO * TR)
    owner_mask = tile_mask.astype(jnp.float32)[:, None]
    return tuple(
        two_products(
            dense,
            left_rows,
            site_all.reshape(WM, WM * PHYS),
            env_all.reshape(WM, RB * RB),
            owned_rows,
            owner_mask,
        )
    )


def solution(mesh):
    in_specs = (
        P(("sector", "grp"), None),
        P("sector"),
        P("grp", "sector", None, None),
        P("grp", "sector", None),
        P("grp", "sector"),
        P("grp", "sector"),
        P("grp", None),
        P("grp", None),
        P("grp", None),
        P("grp", None),
    )
    out_specs = (P(("sector", "grp"), None), P(("sector", "grp"), None))
    return jax.shard_map(local, mesh=mesh, in_specs=in_specs, out_specs=out_specs, check_vma=False)
```

```python
import functools

import jax
import jax.numpy as jnp
from jax import lax
from jax.experimental import pallas as pl
from jax.experimental.pallas import tpu as pltpu
from jax.sharding import PartitionSpec as P

WM = 64
D1 = 4
RB = 32
TR = 128
TPO = 4
CAP = 2
PHYS = 16


epsilon = 1e-06


MESH = pl.DeviceIdType.MESH
SHARE = 16


def send_to(src, dst, send_sem, recv_sem, target):
    return pltpu.make_async_remote_copy(
        src_ref=src,
        dst_ref=dst,
        send_sem=send_sem,
        recv_sem=recv_sem,
        device_id=target,
        device_id_type=MESH,
    )


def greet(chips, chip, core, sectors):
    barrier = pltpu.get_barrier_semaphore()

    def greet_chip(step, carry):
        other = lax.rem(chip + step, chips)
        pl.semaphore_signal(
            barrier, inc=1, device_id={"grp": other * 2 + core}, device_id_type=MESH
        )
        return carry

    lax.fori_loop(1, chips, greet_chip, 0)
    pl.semaphore_signal(
        barrier, inc=1, device_id={"grp": chip * 2 + 1 - core}, device_id_type=MESH
    )
    owner = lax.axis_index("sector")

    def greet_owner(step, carry):
        pl.semaphore_signal(
            barrier,
            inc=1,
            device_id={"sector": lax.rem(owner + step, sectors)},
            device_id_type=MESH,
        )
        return carry

    lax.fori_loop(1, sectors, greet_owner, 0)


def await_greetings(chips, sectors):
    pl.semaphore_wait(pltpu.get_barrier_semaphore(), chips + sectors - 1)


NEAR = 4


def offsets(core):
    return (1, -1, 2 - 4 * core)


def spread(items, chips, chip, core, sems):
    far_count = chips // NEAR
    sibling = {"grp": chip * 2 + 1 - core}
    send_sem, recv_sem, pair_send, pair_recv = sems
    numbers = range(len(items))

    def far(item, step):
        mine = items[item].at[chip, core]
        target = lax.rem(chip + step * NEAR, chips)
        return send_to(
            mine,
            mine,
            send_sem.at[item, step],
            recv_sem.at[item, step],
            {"grp": target * 2 + core},
        )

    def near(item, way, step):
        source = lax.rem(chip + chips - step * NEAR, chips)
        block = items[item].at[source, core]
        target = lax.rem(chip + chips + offsets(core)[way], chips)
        index = (way + 1) * far_count + step
        return send_to(
            block,
            block,
            send_sem.at[item, index],
            recv_sem.at[item, index],
            {"grp": target * 2 + core},
        )

    def forward(item, source, index):
        block = items[item].at[source, core]
        return send_to(
            block, block, pair_send.at[item, index], pair_recv.at[item, index], sibling
        )

    def forward_far(item, step):
        return forward(item, lax.rem(chip + chips - step * NEAR, chips), step)

    def forward_near(item, way, step):
        source = lax.rem(chip + 2 * chips - offsets(core)[way] - step * NEAR, chips)
        return forward(item, source, (way + 1) * far_count + step)

    def far_start(step, carry):
        for item in numbers:
            far(item, step).start()
        return carry

    def far_relay(step, carry):
        for item in numbers:
            far(item, step).wait_recv()
            for way in range(NEAR - 1):
                near(item, way, step).start()
            forward_far(item, step).start()
        return carry

    def near_relay(step, carry):
        for item in numbers:
            for way in range(NEAR - 1):
                near(item, way, step).wait_recv()
                forward_near(item, way, step).start()
        return carry

    def far_finish(step, carry):
        for item in numbers:
            far(item, step).wait_send()
        return carry

    def near_finish(step, carry):
        for item in numbers:
            forward_far(item, step).wait()
            for way in range(NEAR - 1):
                near(item, way, step).wait_send()
                forward_near(item, way, step).wait()
        return carry

    lax.fori_loop(1, far_count, far_start, 0)
    for item in numbers:
        for way in range(NEAR - 1):
            near(item, way, 0).start()
        forward_far(item, 0).start()
    lax.fori_loop(1, far_count, far_relay, 0)
    lax.fori_loop(0, far_count, near_relay, 0)
    lax.fori_loop(1, far_count, far_finish, 0)
    lax.fori_loop(0, far_count, near_finish, 0)


def gather_kernel(
    chips,
    sectors,
    rows_ref,
    site_ref,
    env_ref,
    code_ref,
    rows_out,
    site_out,
    env_out,
    code_out,
    send_sem,
    recv_sem,
    pair_send,
    pair_recv,
    code_sems,
):
    position = lax.axis_index("grp")
    owner = lax.axis_index("sector")
    chip, core = position // 2, lax.rem(position, 2)
    greet(chips, chip, core, sectors)
    for source, target in ((rows_ref, rows_out), (site_ref, site_out), (env_ref, env_out)):
        target[chip, core] = source[...]
    code_out[owner] = code_ref[owner]
    await_greetings(chips, sectors)

    def code_copy(step):
        other = lax.rem(owner + step, sectors)
        return send_to(
            code_ref.at[other],
            code_out.at[owner],
            code_sems.at[0, step],
            code_sems.at[1, step],
            {"sector": other},
        )

    def code_start(step, carry):
        code_copy(step).start()
        return carry

    def code_finish(step, carry):
        code_copy(step).wait()
        return carry

    lax.fori_loop(1, sectors, code_start, 0)
    spread(
        (site_out, env_out, rows_out),
        chips,
        chip,
        core,
        (send_sem, recv_sem, pair_send, pair_recv),
    )
    lax.fori_loop(1, sectors, code_finish, 0)


def gather_all(start_vector, site_right, right_env, codes):
    chips = lax.axis_size("grp") // 2
    sectors = lax.axis_size("sector")
    operands = (start_vector, site_right, right_env)
    return pl.pallas_call(
        functools.partial(gather_kernel, chips, sectors),
        out_shape=[jax.ShapeDtypeStruct((chips, 2) + a.shape, a.dtype) for a in operands]
        + [jax.ShapeDtypeStruct(codes.shape, codes.dtype)],
        in_specs=[pl.BlockSpec(memory_space=pltpu.VMEM)] * 4,
        out_specs=[pl.BlockSpec(memory_space=pltpu.VMEM)] * 4,
        scratch_shapes=[pltpu.SemaphoreType.DMA((3, chips))] * 4
        + [pltpu.SemaphoreType.DMA((2, sectors))],
        compiler_params=pltpu.CompilerParams(collective_id=0, has_side_effects=True),
    )(*operands, codes)


def product(dense_ref, mix_ref, vector, part, base):
    tile = 256

    def one_tile(index, carry):
        rows = pl.ds(pl.multiple_of(index * tile, tile), tile)
        total = jnp.zeros((tile, vector.shape[1]), jnp.float32)
        for channel in range(dense_ref.shape[0]):
            mixed = jnp.dot(
                dense_ref[channel, rows, :], vector, preferred_element_type=jnp.float32
            ).astype(jnp.bfloat16)
            total += jnp.dot(mixed, mix_ref[channel], preferred_element_type=jnp.float32)
        held = tile // (2 * SHARE * NEAR)
        split = total.astype(jnp.bfloat16).reshape(held, NEAR, 2, SHARE, vector.shape[1])
        chunk = pl.ds(index * held, held)
        for kind in range(NEAR):
            part[base, kind, chunk] = split[:, kind, 0]
            part[base + 1, kind, chunk] = split[:, kind, 1]
        return carry

    lax.fori_loop(0, TPO * TR // tile, one_tile, 0)


def reduce_share(chips, chip, core, part, base, sib, ready, near_got, far_ready, far_got, sems, meanwhile=None):
    pair_sems, near_sems, far_sems = sems
    ways = offsets(core)[::-1]
    far_count = chips // NEAR

    def kind_of(way):
        return lax.rem(chip + chips + ways[way], NEAR) if way < NEAR - 1 else lax.rem(chip, NEAR)

    def pair(way):
        kind = kind_of(way)
        return send_to(
            part.at[base + 1 - core, kind],
            sib.at[kind],
            pair_sems.at[0, way],
            pair_sems.at[1, way],
            {"grp": chip * 2 + 1 - core},
        )

    def near(way):
        target = lax.rem(chip + chips + ways[way], chips)
        return send_to(
            ready.at[kind_of(way)],
            near_got.at[way],
            near_sems.at[0, way],
            near_sems.at[1, way],
            {"grp": target * 2 + core},
        )

    def far(step):
        target = lax.rem(chip + step * NEAR, chips)
        return send_to(
            far_ready.at[target // NEAR],
            far_got.at[step],
            far_sems.at[0, step],
            far_sems.at[1, step],
            {"grp": target * 2 + core},
        )

    for way in range(NEAR):
        pair(way).start()
    for way in range(NEAR - 1):
        pair(way).wait_recv()
        kind = kind_of(way)
        ready[kind] = (
            part[base + core, kind].astype(jnp.float32) + sib[kind].astype(jnp.float32)
        ).astype(jnp.bfloat16)
        near(way).start()
    pair(NEAR - 1).wait_recv()
    kind = kind_of(NEAR - 1)
    total = part[base + core, kind].astype(jnp.float32) + sib[kind].astype(jnp.float32)
    if meanwhile is not None:
        meanwhile()
    for way in range(NEAR - 1):
        near(way).wait_recv()
        total += near_got[way].astype(jnp.float32)
    far_ready[...] = total.astype(jnp.bfloat16)
    for step in range(1, far_count):
        far(step).start()
    share = far_ready[chip // NEAR].astype(jnp.float32)
    for step in range(1, far_count):
        far(step).wait_recv()
        share += far_got[step].astype(jnp.float32)
    for way in range(NEAR):
        pair(way).wait_send()
    for way in range(NEAR - 1):
        near(way).wait_send()
    for step in range(1, far_count):
        far(step).wait_send()
    return share


def step_kernel(
    chips,
    sectors,
    dense_ref,
    left_ref,
    site_ref,
    env_ref,
    start_ref,
    mask_ref,
    first_out,
    second_out,
    mix_ref,
    wide_mix,
    part,
    sib,
    ready,
    near_got,
    far_ready,
    far_got,
    held,
    norm_mine,
    norm_got,
    pair_sems,
    near_sems,
    far_sems,
    spread_sems,
    norm_sems,
):
    position = lax.axis_index("grp")
    owner = lax.axis_index("sector")
    chip, core = position // 2, lax.rem(position, 2)
    rows = TPO * TR
    columns = start_ref.shape[-1]
    greet(chips, chip, core, sectors)
    fill_mixing(left_ref, site_ref, env_ref, mix_ref, wide_mix)
    masked = start_ref[...].reshape(rows, columns) * mask_ref[...].astype(jnp.bfloat16)
    product(dense_ref, mix_ref, masked, part, 0)
    await_greetings(chips, sectors)
    share_mask = mask_ref[pl.ds(pl.multiple_of(position * SHARE, SHARE), SHARE), :]
    total = reduce_share(
        chips,
        chip,
        core,
        part,
        0,
        sib.at[0],
        ready.at[0],
        near_got.at[0],
        far_ready.at[0],
        far_got.at[0],
        (pair_sems.at[0], near_sems.at[0], far_sems.at[0]),
    )
    first = (total * share_mask).astype(jnp.bfloat16)
    first_out[...] = first
    held[chip, core] = first
    spread((held,), chips, chip, core, [spread_sems.at[at] for at in range(4)])
    def norm_copy(step):
        return send_to(
            norm_mine,
            norm_got.at[step],
            norm_sems.at[0, step],
            norm_sems.at[1, step],
            {"sector": lax.rem(owner + step, sectors)},
        )

    def norm_start(step, carry):
        norm_copy(step).start()
        return carry

    def norm_collect(step, carry):
        norm_copy(step).wait()
        return carry + norm_got[step]

    def send_norm():
        wide = held[...].reshape(rows, columns).astype(jnp.float32)
        squares = jnp.sum((wide * wide).reshape(rows // 8, 8, columns), axis=0)
        norm_mine[...] = sum(squares[:, at : at + 128] for at in range(0, columns, 128))
        lax.fori_loop(1, sectors, norm_start, 0)

    product(dense_ref, mix_ref, held[...].reshape(rows, columns), part, 2)
    total = reduce_share(
        chips,
        chip,
        core,
        part,
        2,
        sib.at[1],
        ready.at[1],
        near_got.at[1],
        far_ready.at[1],
        far_got.at[1],
        (pair_sems.at[1], near_sems.at[1], far_sems.at[1]),
        send_norm,
    )
    sums = lax.fori_loop(1, sectors, norm_collect, norm_mine[...])
    count = float(sectors * rows * columns)
    inverse_norm = lax.rsqrt(jnp.sum(sums, keepdims=True) / count + epsilon)
    second_out[...] = (total * inverse_norm * share_mask).astype(jnp.bfloat16)


def two_products(dense, left, site, env, owned_rows, owner_mask):
    chips = lax.axis_size("grp") // 2
    sectors = lax.axis_size("sector")
    columns = owned_rows.shape[-1]
    shares = (chips // NEAR, SHARE, columns)
    share = jax.ShapeDtypeStruct((SHARE, columns), jnp.bfloat16)
    return pl.pallas_call(
        functools.partial(step_kernel, chips, sectors),
        out_shape=[share, share],
        in_specs=[pl.BlockSpec(memory_space=pltpu.VMEM)] * 6,
        out_specs=[pl.BlockSpec(memory_space=pltpu.VMEM)] * 2,
        scratch_shapes=[
            pltpu.VMEM(dense.shape, jnp.bfloat16),
            pltpu.VMEM((dense.shape[0] * D1, D1 * RB, columns), jnp.float32),
            pltpu.VMEM((4, NEAR) + shares, jnp.bfloat16),
            pltpu.VMEM((2, NEAR) + shares, jnp.bfloat16),
            pltpu.VMEM((2, NEAR) + shares, jnp.bfloat16),
            pltpu.VMEM((2, NEAR - 1) + shares, jnp.bfloat16),
            pltpu.VMEM((2,) + shares, jnp.bfloat16),
            pltpu.VMEM((2,) + shares, jnp.bfloat16),
            pltpu.VMEM((chips, 2, SHARE, columns), jnp.bfloat16),
            pltpu.VMEM((8, 128), jnp.float32),
            pltpu.VMEM((sectors, 8, 128), jnp.float32),
            pltpu.SemaphoreType.DMA((2, 2, NEAR)),
            pltpu.SemaphoreType.DMA((2, 2, NEAR)),
            pltpu.SemaphoreType.DMA((2, 2, chips // NEAR)),
            pltpu.SemaphoreType.DMA((4, 1, chips)),
            pltpu.SemaphoreType.DMA((2, sectors)),
        ],
        compiler_params=pltpu.CompilerParams(
            collective_id=1, has_side_effects=True, vmem_limit_bytes=40 * 1024 * 1024
        ),
    )(dense, left, site, env, owned_rows, owner_mask)


def pack_kernel(pick_ref, env_ref, out_ref):
    def one_slot(slot, carry):
        pick = pick_ref[slot]

        @pl.when(pick > 0)
        def _():
            out_ref[slot] = env_ref[pick - 1]

        @pl.when(pick <= 0)
        def _():
            out_ref[slot] = jnp.zeros_like(out_ref[slot])

        return carry

    lax.fori_loop(0, out_ref.shape[0], one_slot, 0)


def pack(pick, blocks):
    return pl.pallas_call(
        pack_kernel,
        out_shape=jax.ShapeDtypeStruct((pick.shape[0], TR, TR), blocks.dtype),
        in_specs=[
            pl.BlockSpec(memory_space=pltpu.SMEM),
            pl.BlockSpec(memory_space=pltpu.VMEM),
        ],
        out_specs=pl.BlockSpec(memory_space=pltpu.VMEM),
    )(pick, blocks)


def assemble_kernel(code_ref, blocks_ref, out_ref, total):
    total[...] = jnp.zeros_like(total)
    channels = out_ref.shape[0]

    def one_slot(slot, carry):
        code = code_ref[slot // (channels * CAP), 0, lax.rem(slot, channels * CAP)]
        channel = lax.rem(slot // CAP, channels)

        @pl.when(code > 0)
        def _():
            place = channel * TPO * TPO + code - 1
            total[place] = total[place] + blocks_ref[slot].astype(jnp.float32)

        return carry

    lax.fori_loop(0, blocks_ref.shape[0], one_slot, 0)
    for channel in range(channels):
        for row in range(TPO):
            for col in range(TPO):
                out_ref[channel, row * TR : (row + 1) * TR, col * TR : (col + 1) * TR] = total[
                    (channel * TPO + row) * TPO + col
                ].astype(out_ref.dtype)


def assemble(codes, blocks, channels):
    return pl.pallas_call(
        assemble_kernel,
        out_shape=jax.ShapeDtypeStruct((channels, TPO * TR, TPO * TR), jnp.bfloat16),
        in_specs=[
            pl.BlockSpec(memory_space=pltpu.SMEM),
            pl.BlockSpec(memory_space=pltpu.VMEM),
        ],
        out_specs=pl.BlockSpec(memory_space=pltpu.VMEM),
        scratch_shapes=[pltpu.VMEM((channels * TPO * TPO, TR, TR), jnp.float32)],
    )(codes, blocks)


def fill_mixing(left_ref, site_ref, env_ref, out_ref, wide):
    group = D1 * WM
    joined = jnp.concatenate(
        [
            jnp.dot(
                left_ref[...],
                site_ref[:, d * group : (d + 1) * group],
                preferred_element_type=jnp.float32,
            )
            for d in range(D1)
        ],
        axis=0,
    ).astype(jnp.bfloat16)
    lanes = D1 * RB
    held = out_ref.shape[0] * D1
    source = lax.broadcasted_iota(jnp.int32, (lanes, D1 * lanes), 0)
    column = lax.broadcasted_iota(jnp.int32, (lanes, D1 * lanes), 1)
    repeat = jnp.where(
        source == (column // lanes) * RB + lax.rem(column, RB), 1.0, 0.0
    ).astype(jnp.bfloat16)
    piece = lax.rem(lax.broadcasted_iota(jnp.int32, (WM, D1 * lanes), 1), lanes) // RB
    for tile in range(RB // D1):
        spread_env = jnp.dot(
            env_ref[:, tile * lanes : (tile + 1) * lanes],
            repeat,
            preferred_element_type=jnp.float32,
        )
        stacked = jnp.concatenate(
            [jnp.where(piece == b, spread_env, 0.0) for b in range(D1)], axis=0
        ).astype(jnp.bfloat16)
        result = jnp.dot(joined, stacked, preferred_element_type=jnp.float32)
        for d in range(D1):
            for a in range(D1):
                at = (d * D1 + a) * held
                for k in range(D1):
                    wide[:, d * RB + tile * D1 + k, a * lanes : (a + 1) * lanes] = result[
                        at : at + held, k * lanes : (k + 1) * lanes
                    ]
    for channel in range(out_ref.shape[0]):
        out_ref[channel] = (
            wide[channel * D1 : (channel + 1) * D1]
            .reshape(out_ref.shape[1], out_ref.shape[2])
            .astype(out_ref.dtype)
        )


def local(
    start_vector,
    tile_live,
    env_blocks,
    block_owner,
    block_rows,
    block_cols,
    site_left,
    mpo_pattern,
    site_right,
    right_env,
):
    sectors = lax.axis_size("sector")
    channels = env_blocks.shape[0]
    held_blocks = env_blocks.shape[1]
    site_local = (
        site_right.reshape(channels, WM, D1, D1).transpose(0, 3, 2, 1).reshape(channels, WM * PHYS)
    )
    left_site = (
        site_left.reshape(channels, WM, D1, D1) * mpo_pattern.astype(jnp.bfloat16)[:, :, None, None]
    )
    left_rows = left_site.transpose(2, 0, 3, 1).reshape(D1 * channels * D1, WM)
    owners = block_owner[:, :, 0]
    owner_hot = (owners[:, :, None] == jnp.arange(sectors, dtype=jnp.int32)[None, None, :]).astype(
        jnp.int32
    )
    position = jnp.sum((jnp.cumsum(owner_hot, axis=1) - owner_hot) * owner_hot, axis=2)
    slot_index = owners * CAP + position
    select = slot_index[:, :, None] == jnp.arange(sectors * CAP, dtype=jnp.int32)[None, None, :]
    chosen = select.astype(jnp.int32)

    def by_owner(values):
        return values.reshape(channels, sectors, CAP).transpose(1, 0, 2)

    block_number = jnp.arange(1, 1 + channels * held_blocks, dtype=jnp.int32)
    pick = by_owner(
        jnp.sum(chosen * block_number.reshape(channels, held_blocks)[:, :, None], axis=1)
    )
    slot_codes = by_owner(
        jnp.sum(chosen * (1 + block_rows * TPO + block_cols)[:, :, None], axis=1)
    )
    slots = channels * CAP
    packed = pack(
        pick.reshape(sectors * slots), env_blocks.reshape(channels * held_blocks, TR, TR)
    )
    got_blocks = lax.all_to_all(
        packed.reshape(sectors, slots, TR, TR),
        "sector",
        split_axis=0,
        concat_axis=0,
        tiled=True,
    )
    owned_rows, site_all, env_all, got_codes = gather_all(
        start_vector, site_local, right_env, slot_codes.reshape(sectors, 1, slots)
    )
    dense = assemble(
        got_codes, got_blocks.reshape(sectors * slots, TR, TR), channels
    )
    tile_mask = (jnp.arange(TR, dtype=jnp.int32)[None, :] < tile_live[:, None]).reshape(TPO * TR)
    owner_mask = tile_mask.astype(jnp.float32)[:, None]
    return tuple(
        two_products(
            dense,
            left_rows,
            site_all.reshape(WM, WM * PHYS),
            env_all.reshape(WM, RB * RB),
            owned_rows,
            owner_mask,
        )
    )


def solution(mesh):
    in_specs = (
        P(("sector", "grp"), None),
        P("sector"),
        P("grp", "sector", None, None),
        P("grp", "sector", None),
        P("grp", "sector"),
        P("grp", "sector"),
        P("grp", None),
        P("grp", None),
        P("grp", None),
        P("grp", None),
    )
    out_specs = (P(("sector", "grp"), None), P(("sector", "grp"), None))
    return jax.shard_map(local, mesh=mesh, in_specs=in_specs, out_specs=out_specs, check_vma=False)
```
